128 devices in a mesh: row: 16 (over z, x), col: 8 (over y, core).
Axes of the slice: x: 4, y: 4, z: 4, core: 2. Of those that a mesh axis runs over, the one named last changes fastest.
Arguments:
- density: bfloat16 [192, 24, 128, 128], P('row'), may hold values from -4 to 4
- slot_cols: int32 [192, 24], replicated, may hold values from -1 to 191, as said below
Outputs:
- purified: bfloat16 [192, 24, 128, 128], P('row', 'col')
The draws below stay inside these ranges and needn't reach their ends.
Inputs may be any that keep to these rules, and one draw needn't show every extreme that they name: `slot_cols`: slots c * 3 to c * 3 + 2 of a block row name distinct block columns of c * 24 to c * 24 + 23, or -1. Within one such range of slots, block rows t * 12 to t * 12 + 11 have at most 28 occupied slots together, exactly 28 for some t and c.
All inputs are finite; a program needn't handle non-finite values.
Results may differ from the reference program's by a relative error of at most 0.0047.
Values may be sent and summed in bfloat16 or wider, within the bound.
A program may use at most 192 MiB of HBM per device.

```python
import jax
import jax.numpy as jnp
from jax import lax

BLOCK = 128
BR_DEV = 12
ROWCAP = 3
NB = 192
GROUP = 24
SLOTS = 24
TILECAP = 28


def draw_slot_cols(key, part):
    tiles_down = NB // BR_DEV
    tiles_across = SLOTS // ROWCAP
    cell_count = BR_DEV * ROWCAP
    key_total, key_cells, key_cols, key_row, key_col = jax.random.split(key, 5)
    totals = jax.random.randint(key_total, (tiles_down, tiles_across), (TILECAP + 1) // 2, TILECAP + 1)
    full_row = jax.random.randint(key_row, (), 0, tiles_down)
    full_col = jax.random.randint(key_col, (), 0, tiles_across)
    down_index = jnp.arange(tiles_down, dtype=jnp.int32)[:, None]
    across_index = jnp.arange(tiles_across, dtype=jnp.int32)[None, :]
    forced = (down_index == full_row) | (across_index == full_col)
    totals = jnp.where(forced, TILECAP, totals)
    scores = jax.random.randint(key_cells, (tiles_down, tiles_across, cell_count), 0, 1 << 20) * cell_count + jnp.arange(cell_count, dtype=jnp.int32)
    ranking = jnp.argsort(jnp.argsort(scores, axis=-1), axis=-1)
    occupied = ranking < totals[:, :, None]
    occupied = occupied.reshape(tiles_down, tiles_across, BR_DEV, ROWCAP).transpose(0, 2, 1, 3).reshape(NB, SLOTS)
    col_scores = jax.random.randint(key_cols, (NB, tiles_across, GROUP), 0, 1 << 20) * GROUP + jnp.arange(GROUP, dtype=jnp.int32)
    chosen = jnp.argsort(col_scores, axis=-1)[:, :, :ROWCAP]
    columns = chosen + jnp.arange(tiles_across, dtype=jnp.int32)[None, :, None] * GROUP
    columns = columns.reshape(NB, SLOTS).astype(jnp.int32)
    return jnp.where(occupied, columns, -1).astype(jnp.int32)


def steps_of(rng, extent, cuts, low, largest):
    factor_of = 1.0
    for position, shards_of in cuts:
        draws = jax.random.uniform(jax.random.fold_in(jax.random.fold_in(rng, 6), position), (shards_of,), jnp.float32, low / len(cuts), largest / len(cuts))
        factor_of = factor_of * jnp.repeat(jnp.exp(draws), extent[position] // shards_of).reshape((-1,) + (1,) * (len(extent) - 1 - position))
    return factor_of


def scatter_about(rng, extent, scale, reach, pieces=(), held_as=jnp.bfloat16):
    array = scale * jax.random.normal(rng, extent, jnp.float32)
    if pieces:
        array = array * steps_of(rng, extent, pieces, -0.22, 0.18)
    return jnp.clip(array, -reach, reach).astype(held_as)


def setup_inputs(seed: int = 0) -> dict:
    splits = jax.random.split(jax.random.key(seed), 3)
    return {
        "density": scatter_about(splits[0], (NB, SLOTS, BLOCK, BLOCK), ((BLOCK * 1.5) ** -0.25), 4.0, ((0, 16),)),
        "slot_cols": draw_slot_cols(jax.random.fold_in(splits[2], 71), 0),
    }


def positions_of(slot_cols):
    targets = jnp.arange(NB, dtype=jnp.int32)
    matches = (slot_cols[:, :, None] == targets[None, None, :]).astype(jnp.int32)
    found_any = jnp.sum(matches, axis=1) > 0
    slot_sum = jnp.sum(matches * jnp.arange(SLOTS, dtype=jnp.int32)[None, :, None], axis=1)
    return jnp.where(found_any, slot_sum, -1).astype(jnp.int32)


def contract(left_blocks, right_blocks, slot_cols, positions):
    def one_row(inputs):
        left_row, row_cols = inputs
        safe_cols = jnp.maximum(row_cols, 0).astype(jnp.int32)
        slot_pick = positions[safe_cols[None, :], safe_cols[:, None]]
        usable = (row_cols[:, None] >= 0) & (row_cols[None, :] >= 0) & (slot_pick >= 0)
        picked = right_blocks[safe_cols[None, :], jnp.maximum(slot_pick, 0).astype(jnp.int32)].astype(jnp.float32)
        picked = picked * usable[:, :, None, None].astype(jnp.float32)
        return jnp.einsum("tab,stbc->sac", left_row.astype(jnp.float32), picked)

    return lax.map(one_row, (left_blocks, slot_cols))


def reference(density, slot_cols):
    occupied = slot_cols >= 0
    masked = density * occupied[:, :, None, None].astype(jnp.bfloat16)
    positions = positions_of(slot_cols)
    square = contract(masked, masked, slot_cols, positions)
    square_half = square.astype(jnp.bfloat16)
    cube_term = contract(square_half, masked, slot_cols, positions)
    return (3.0 * square - 2.0 * cube_term).astype(jnp.bfloat16)
```

```python
import functools
import math

import jax
import jax.numpy as jnp
from jax import lax
from jax.experimental import pallas as pl
from jax.experimental.pallas import tpu as pltpu
from jax.sharding import PartitionSpec as P

F32 = jnp.float32
BF16 = jnp.bfloat16
I32 = jnp.int32
CAP1 = 40
CAP2 = 48
JOB = 1024
MESH = pl.DeviceIdType.MESH


def fdiv(x, n):
    return jnp.floor((x + 0.5) * (1.0 / n))


def mm(a, b, contract=((1,), (0,))):
    return lax.dot_general(
        a.astype(BF16), b.astype(BF16), (contract, ((), ())), preferred_element_type=F32
    )


NT = ((1,), (1,))


def ones_where(cond):
    return jnp.where(cond, 1.0, 0.0).astype(F32)


def plan_body(rc_ref, cols_ref, src1_ref, src2_ref, jobs_ref, flag_ref, own_ref, *, dims):
    side, band_rows, width, per = dims
    count, slots = cols_ref.shape
    row_here, col_here = rc_ref[0], rc_ref[1]
    odd = lax.rem(col_here, 2)
    hi_here = row_here // side
    lo_here = lax.rem(row_here, side)
    p_here = jnp.where(odd == 0, lo_here, hi_here)
    q_here = jnp.where(odd == 0, hi_here, lo_here)
    odd_f = odd.astype(F32)
    p_f, q_f = p_here.astype(F32), q_here.astype(F32)

    square = (count, count)
    row_at = lax.broadcasted_iota(I32, square, 0).astype(F32)
    lane_at = lax.broadcasted_iota(I32, square, 1).astype(F32)
    group = fdiv(lane_at, width)

    def coords(index):
        band = fdiv(index, band_rows)
        hi = fdiv(band, side)
        lo = band - side * hi
        p = odd_f * hi + (1.0 - odd_f) * lo
        q = odd_f * lo + (1.0 - odd_f) * hi
        p = p - p_f
        q = q - q_f
        return band, p + side * ones_where(p < 0.0), q + side * ones_where(q < 0.0)

    band, prel, qrel = coords(row_at)
    band_lane, _, qrel_lane = coords(lane_at)
    own_row = row_at - band_rows * band

    slot_row = lax.broadcasted_iota(I32, (slots, count), 0).astype(F32)
    slot_lane = lax.broadcasted_iota(I32, (slots, count), 1).astype(F32)
    cols = cols_ref[...].astype(F32)
    occupied = jnp.zeros(square, F32)
    slot = per * group
    for u in range(per):
        expand = ones_where(slot_row == per * fdiv(slot_lane, width) + u)
        hit = ones_where(mm(cols, expand) == lane_at)
        occupied = occupied + hit
        slot = slot + u * hit
    own_ref[...] = jnp.where(occupied > 0.0, slot, -1.0)

    in_group = ones_where(group == col_here.astype(F32))
    part = occupied * in_group
    shared = mm(part, part, NT)
    wanted = occupied * jnp.maximum(in_group, ones_where(shared > 0.0))
    identity = ones_where(row_at == lane_at)
    flipped = mm(identity, occupied, NT)
    wanted_b = wanted.astype(BF16)

    def needed_by(d, e):
        pd, qe = lax.rem(p_here + d, side), lax.rem(q_here + e, side)
        who = jnp.where(odd == 0, qe * side + pd, pd * side + qe).astype(F32)
        picked = flipped * ones_where(band_lane == who)
        return occupied * ones_where(mm(picked, wanted_b) > 0.0)

    before = ones_where(row_at < lane_at)
    in_band = ones_where((lane_at < row_at) & (band_lane == band))
    in_class = ones_where((lane_at < row_at) & (qrel_lane == qrel))
    everything = jnp.ones(square, BF16)

    def rank_of(need, earlier):
        return mm(need, before) + mm(mm(earlier, need), everything)

    class_row = lax.broadcasted_iota(I32, (8, count), 0).astype(F32)
    _, _, class_of = coords(lax.broadcasted_iota(I32, (8, count), 1).astype(F32))
    classes = ones_where(class_of == class_row)
    most1 = jnp.zeros((1, count), F32)
    most2 = jnp.zeros((8, 1), F32)
    union, direct = [], []
    for d in range(side):
        total = None
        for e in range(side):
            need = needed_by(d, e)
            sums = jnp.sum(mm(classes, need), axis=1, keepdims=True)
            sums = sums * ones_where(class_row[:, :1] != float(e))
            most2 = jnp.maximum(most2, sums)
            total = need if total is None else jnp.maximum(total, need)
            if d == 0:
                direct.append(need)
        union.append(total)
    rank1, rank2 = [], []
    for d in range(side):
        rank = rank_of(union[d], in_band)
        rank1.append(rank)
        used = (rank + 1.0) * union[d] * ones_where(prel != float(d))
        most1 = jnp.maximum(most1, jnp.max(used, axis=0, keepdims=True))
        rank2.append(rank_of(direct[d], in_class))
    over1 = jnp.max(most1, axis=1, keepdims=True) > float(CAP1)
    over2 = jnp.max(most2, axis=0, keepdims=True) > float(CAP2)
    over = jnp.where(over1 | over2, 1, 0).astype(I32)
    flag_ref[...] = jnp.broadcast_to(over, flag_ref.shape)

    def invert(rank, value_hi, value_lo, cap):
        rows = []
        value = 64.0 * value_hi + value_lo
        for n in range(cap):
            rows.append(jnp.sum(jnp.where(rank == float(n + 1), value, 0.0), axis=0, keepdims=True))
        return jnp.concatenate(rows, axis=0)

    def to_lanes(stack):
        ones = jnp.ones((8, stack.shape[1]), F32)
        return lax.dot_general(
            ones, stack, (NT, ((), ())), preferred_element_type=F32, precision=lax.Precision.HIGHEST
        )

    sel_row = lax.broadcasted_iota(I32, (16, count), 0).astype(F32)
    sel_lane = lax.broadcasted_iota(I32, (16, count), 1).astype(F32)
    first = (row_here * band_rows).astype(F32)
    pick = ones_where((sel_lane == sel_row + first) & (sel_row < float(band_rows)))
    slot16 = mm(pick, slot)
    place = sel_row * slots + slot16
    zeros16 = jnp.zeros_like(place)
    stacks = []
    for d in range(1, side):
        rank = mm(pick, jnp.minimum((rank1[d] + 1.0) * union[d], 255.0))
        stacks.append(invert(rank, zeros16, place, CAP1))
    src1 = to_lanes(jnp.concatenate(stacks, axis=0))
    src1_ref[...] = src1.astype(I32)

    in_recv1 = (prel - 1.0) * CAP1 + jnp.minimum(rank1[0], CAP1 - 1.0)
    in_band_at = own_row * slots + slot
    after1 = jnp.where(prel == 0.0, (side - 1.0) * CAP1 + in_band_at, in_recv1)
    members = side * band_rows
    mem_row = lax.broadcasted_iota(I32, (members, count), 0).astype(F32)
    mem_lane = lax.broadcasted_iota(I32, (members, count), 1).astype(F32)
    mem_band, mem_p, mem_q = coords(mem_lane)
    pick = ones_where(
        (mem_q == 0.0) & (mem_p * band_rows + (mem_lane - band_rows * mem_band) == mem_row)
    )
    after_hi = fdiv(after1, 64)
    hi48 = mm(pick, after_hi)
    lo48 = mm(pick, after1 - 64.0 * after_hi)
    stacks = []
    for e in range(1, side):
        rank = mm(pick, jnp.minimum((rank2[e] + 1.0) * direct[e], 255.0))
        stacks.append(invert(rank, hi48, lo48, CAP2))
    src2 = to_lanes(jnp.concatenate(stacks, axis=0))
    src2_ref[...] = src2.astype(I32)

    held = band_rows * slots
    loc = jnp.where(
        prel + qrel == 0.0,
        in_band_at,
        jnp.where(
            qrel == 0.0,
            held + in_recv1,
            held + (side - 1.0) * CAP1 + (qrel - 1.0) * CAP2 + jnp.minimum(rank2[0], CAP2 - 1.0),
        ),
    )
    loc_hi = fdiv(loc, 64)
    loc_lo = (loc - 64.0 * loc_hi).astype(BF16)
    loc_hi = loc_hi.astype(BF16)
    occ_b = occupied.astype(BF16)
    small = (slots, count)
    t_at = lax.broadcasted_iota(I32, small, 0).astype(F32)
    wide_at = lax.broadcasted_iota(I32, (128, count), 0).astype(F32)
    pack = 4
    wide_i = fdiv(wide_at, 128 // pack)
    wide_t = wide_at - (128 // pack) * wide_i
    tri = ones_where(
        lax.broadcasted_iota(I32, (slots, slots), 1) < lax.broadcasted_iota(I32, (slots, slots), 0)
    )
    t_out = lax.broadcasted_iota(I32, (slots, 128), 0).astype(F32)
    wanted_rows = mm(jnp.where(sel_row + first == sel_lane, 1.0, 0.0), wanted)
    for g in range(band_rows // pack):
        exists = jnp.zeros((slots, 128), F32)
        at_hi = jnp.zeros((slots, 128), F32)
        at_lo = jnp.zeros((slots, 128), F32)
        for ii in range(pack):
            i = g * pack + ii
            line = own_ref[pl.ds(row_here * band_rows + i, 1), :]
            left = ones_where(t_at == line).astype(BF16)
            right = ones_where((wide_i == float(ii)) & (wide_t == line))
            right = (right * wanted_rows[i : i + 1, :]).astype(BF16)
            exists = exists + mm(mm(left, occ_b), right, NT)
            at_hi = at_hi + mm(mm(left, loc_hi), right, NT)
            at_lo = at_lo + mm(mm(left, loc_lo), right, NT)
        rank = jnp.where(exists > 0.0, mm(tri, exists), -1.0)
        code = t_out * JOB + at_hi * 64.0 + at_lo
        rows = []
        for n in range(slots):
            rows.append(jnp.sum(jnp.where(rank == float(n), code, 0.0), axis=0, keepdims=True))
        rows.append(jnp.sum(exists, axis=0, keepdims=True))
        flags = jnp.zeros((1, 128), F32)
        for ii in range(pack):
            i = g * pack + ii
            line = own_ref[pl.ds(row_here * band_rows + i, 1), :]
            right = ones_where((wide_i == float(ii)) & (wide_t == line)).astype(BF16)
            mark = jnp.broadcast_to(wanted_rows[i : i + 1, :], (8, count))
            flags = flags + mm(mark, right, NT)[:1]
        rows.append(flags)
        rows.append(jnp.zeros((32 - slots - 2, 128), F32))
        jobs_ref[g] = jnp.concatenate(rows, axis=0).astype(I32)


def make_plan(rc, cols, dims):
    side, band_rows, _, _ = dims
    count = cols.shape[0]
    groups = band_rows // 4
    return pl.pallas_call(
        functools.partial(plan_body, dims=dims),
        out_shape=(
            jax.ShapeDtypeStruct((8, (side - 1) * CAP1), I32),
            jax.ShapeDtypeStruct((8, (side - 1) * CAP2), I32),
            jax.ShapeDtypeStruct((groups, 32, 128), I32),
            jax.ShapeDtypeStruct((8, 128), I32),
        ),
        in_specs=[
            pl.BlockSpec(memory_space=pltpu.SMEM),
            pl.BlockSpec(memory_space=pltpu.VMEM),
        ],
        out_specs=[pl.BlockSpec(memory_space=pltpu.VMEM)] * 4,
        scratch_shapes=[pltpu.VMEM((count, count), F32)],
        name="plan",
    )(rc, cols)


def gather_body(index_ref, *refs, sizes):
    sources, out_ref, sem = refs[: len(sizes)], refs[len(sizes)], refs[-1]
    total = out_ref.shape[0]

    def issue(n, carry):
        at = index_ref[0, n]
        start = 0
        for ref, size in zip(sources, sizes):
            inside = (at >= start) & (at < start + size)

            @pl.when(inside)
            def _(ref=ref, start=start):
                pltpu.make_async_copy(ref.at[at - start], out_ref.at[n], sem).start()

            start += size
        return carry

    lax.fori_loop(0, total, issue, 0, unroll=4)
    pltpu.make_async_copy(out_ref, out_ref, sem).wait()


def gather(index, total, *sources):
    block = sources[0].shape[1:]
    return pl.pallas_call(
        functools.partial(gather_body, sizes=tuple(s.shape[0] for s in sources)),
        out_shape=jax.ShapeDtypeStruct((total, *block), sources[0].dtype),
        in_specs=[pl.BlockSpec(memory_space=pltpu.SMEM)]
        + [pl.BlockSpec(memory_space=pl.ANY)] * len(sources),
        out_specs=pl.BlockSpec(memory_space=pltpu.VMEM),
        scratch_shapes=[pltpu.SemaphoreType.DMA],
        name="gather",
    )(index, *sources)


def ring_body(*refs, side, cols, stage, flags):
    if flags:
        send_ref, flag_ref, recv_ref, heard_ref = refs[:4]
    else:
        send_ref, recv_ref = refs[:2]
    relay_up, relay_down, send_sem, recv_sem = refs[-4:]
    row, col = lax.axis_index("row"), lax.axis_index("col")
    hi, lo = row // side, lax.rem(row, side)
    low_axis = lax.rem(col + stage, 2)

    def along(d):
        by_lo = hi * side + lax.rem(lo + d, side)
        by_hi = lax.rem(hi + d, side) * side + lo
        return (by_lo * (1 - low_axis) + by_hi * low_axis, col)

    right, left = along(1), along(side - 1)
    peers = [(row, lax.rem(col + k, cols)) for k in range(1, cols)] if flags else []
    barrier = pltpu.get_barrier_semaphore()
    for peer in [right, left, *peers]:
        pl.semaphore_signal(barrier, inc=1, device_id=peer, device_id_type=MESH)
    pl.semaphore_wait(barrier, 2 + len(peers))

    half = send_ref.shape[1] // 2
    lower, upper = pl.ds(0, half), pl.ds(half, half)

    def copy(n, src, dst, peer):
        return pltpu.make_async_remote_copy(
            src_ref=src,
            dst_ref=dst,
            send_sem=send_sem.at[n],
            recv_sem=recv_sem.at[n],
            device_id=peer,
            device_id_type=MESH,
        )

    far_up = copy(0, send_ref.at[1, lower], relay_up, right)
    far_down = copy(1, send_ref.at[1, upper], relay_down, left)
    near_up = copy(2, send_ref.at[0], recv_ref.at[2], right)
    near_down = copy(3, send_ref.at[2], recv_ref.at[0], left)
    next_up = copy(4, relay_up, recv_ref.at[1, lower], right)
    next_down = copy(5, relay_down, recv_ref.at[1, upper], left)
    told = [copy(6 + k, flag_ref, heard_ref.at[k], peer) for k, peer in enumerate(peers)]
    far_up.start()
    far_down.start()
    near_up.start()
    near_down.start()
    for one in told:
        one.start()
    far_up.wait_recv()
    next_up.start()
    far_down.wait_recv()
    next_down.start()
    far_up.wait_send()
    far_down.wait_send()
    for one in told:
        one.wait()
    near_up.wait()
    near_down.wait()
    next_up.wait()
    next_down.wait()


def ring(send, flag, side, cols, stage):
    three, cap, *block = send.shape
    flags = flag is not None
    copies = 6 + (cols - 1 if flags else 0)
    out_shape = [jax.ShapeDtypeStruct(send.shape, send.dtype)]
    if flags:
        out_shape.append(jax.ShapeDtypeStruct((cols - 1, *flag.shape), flag.dtype))
    return pl.pallas_call(
        functools.partial(ring_body, side=side, cols=cols, stage=stage, flags=flags),
        out_shape=out_shape,
        in_specs=[pl.BlockSpec(memory_space=pl.ANY)] * (2 if flags else 1),
        out_specs=[pl.BlockSpec(memory_space=pl.ANY)] * len(out_shape),
        scratch_shapes=[
            pltpu.VMEM((cap // 2, *block), send.dtype),
            pltpu.VMEM((cap // 2, *block), send.dtype),
            pltpu.SemaphoreType.DMA((copies,)),
            pltpu.SemaphoreType.DMA((copies,)),
        ],
        compiler_params=pltpu.CompilerParams(collective_id=stage, has_side_effects=True),
        name="ring",
    )(*([send, flag] if flags else [send]))


def products_body(rc_ref, jobs_ref, band_ref, recv1_ref, recv2_ref, out_ref, held, half, square, sem, *, per):
    n_band, n1, n2 = band_ref.shape[0], recv1_ref.shape[0], recv2_ref.shape[0]
    copies = [
        pltpu.make_async_copy(band_ref, held.at[pl.ds(0, n_band)], sem.at[0]),
        pltpu.make_async_copy(recv1_ref, held.at[pl.ds(n_band, n1)], sem.at[1]),
        pltpu.make_async_copy(recv2_ref, held.at[pl.ds(n_band + n1, n2)], sem.at[2]),
    ]
    for one in copies:
        one.start()
    col_here = rc_ref[1]
    rows = out_ref.shape[0]
    slots = n_band // rows
    block = out_ref.shape[2:]
    for one in copies:
        one.wait()

    def job(i, t):
        return i // 4, lax.rem(i, 4) * 32 + t

    def summed(left, i, t):
        g, lane = job(i, t)

        def step(q, acc):
            code = jobs_ref[g, q, lane]
            at = lax.rem(code, JOB)
            return acc + jnp.dot(
                left[i * slots + code // JOB], held[at], preferred_element_type=F32
            )

        return lax.fori_loop(0, jobs_ref[g, slots, lane], step, jnp.zeros(block, F32))

    def first(n, carry):
        i, t = n // slots, lax.rem(n, slots)
        g, lane = job(i, t)

        @pl.when(jobs_ref[g, slots + 1, lane] > 0)
        def _():
            total = summed(held, i, t)
            half[n] = total.astype(BF16)
            s = t - col_here * per

            @pl.when((s >= 0) & (s < per))
            def _():
                square[i * per + s] = total

        return carry

    lax.fori_loop(0, n_band, first, 0)

    def second(n, carry):
        i, s = n // per, lax.rem(n, per)
        t = col_here * per + s
        g, lane = job(i, t)
        wanted = jobs_ref[g, slots + 1, lane] > 0

        @pl.when(wanted)
        def _():
            cube = summed(half, i, t)
            out_ref[i, s] = (3.0 * square[n] - 2.0 * cube).astype(BF16)

        @pl.when(jnp.logical_not(wanted))
        def _():
            out_ref[i, s] = jnp.zeros(block, BF16)

        return carry

    lax.fori_loop(0, rows * per, second, 0)


def products(rc, jobs, band, recv1, recv2, rows, per):
    block = band.shape[1:]
    return pl.pallas_call(
        functools.partial(products_body, per=per),
        out_shape=jax.ShapeDtypeStruct((rows, per, *block), BF16),
        in_specs=[pl.BlockSpec(memory_space=pltpu.SMEM)] * 2
        + [pl.BlockSpec(memory_space=pl.ANY)] * 3,
        out_specs=pl.BlockSpec(memory_space=pltpu.VMEM),
        scratch_shapes=[
            pltpu.VMEM((band.shape[0] + recv1.shape[0] + recv2.shape[0], *block), BF16),
            pltpu.VMEM(band.shape, BF16),
            pltpu.VMEM((rows * per, *block), F32),
            pltpu.SemaphoreType.DMA((3,)),
        ],
        compiler_params=pltpu.CompilerParams(vmem_limit_bytes=60 * 1024 * 1024),
        name="products",
    )(rc, jobs, band, recv1, recv2)


def spread_body(x_ref, out_ref, send_sem, recv_sem, *, axis, size):
    row, col = lax.axis_index("row"), lax.axis_index("col")

    def peer(k):
        if axis == "row":
            return (lax.rem(row + k, size), col)
        return (row, lax.rem(col + k, size))

    barrier = pltpu.get_barrier_semaphore()
    for k in range(1, size):
        pl.semaphore_signal(barrier, inc=1, device_id=peer(k), device_id_type=MESH)
    pl.semaphore_wait(barrier, size - 1)
    copies = []
    for k in range(1, size):
        one = pltpu.make_async_remote_copy(
            src_ref=x_ref,
            dst_ref=out_ref.at[k - 1],
            send_sem=send_sem.at[k - 1],
            recv_sem=recv_sem.at[k - 1],
            device_id=peer(k),
            device_id_type=MESH,
        )
        one.start()
        copies.append(one)
    for one in copies:
        one.wait()


def spread(x, axis, size, collective_id):
    others = pl.pallas_call(
        functools.partial(spread_body, axis=axis, size=size),
        out_shape=jax.ShapeDtypeStruct((size - 1, *x.shape), x.dtype),
        in_specs=[pl.BlockSpec(memory_space=pl.ANY)],
        out_specs=pl.BlockSpec(memory_space=pl.ANY),
        scratch_shapes=[pltpu.SemaphoreType.DMA((size - 1,)), pltpu.SemaphoreType.DMA((size - 1,))],
        compiler_params=pltpu.CompilerParams(collective_id=collective_id, has_side_effects=True),
        name="spread",
    )(x)
    return jnp.concatenate([x[None], others], axis=0)


def dense_body(rc_ref, cols_ref, left_ref, panel_ref, out_ref, left, right, acc, sem, *, dims, mixed):
    side, band_rows, _, per = dims
    slots = cols_ref.shape[1]
    row_here, col_here = rc_ref[0], rc_ref[1]
    tile = band_rows * per
    row_count, col_count = side * side, slots // per

    def one_out(n, carry):
        i, s = n // per, lax.rem(n, per)
        target = cols_ref[row_here * band_rows + i, col_here * per + s]
        acc[...] = jnp.zeros_like(acc)

        def one_t(t, carry):
            k = cols_ref[row_here * band_rows + i, t]
            safe = jnp.maximum(k, 0)
            away = lax.rem(row_here - safe // band_rows + row_count, row_count)
            if mixed:
                back = lax.rem(col_here - t // per + col_count, col_count)
                at_left = back * tile + i * per + lax.rem(t, per)
            else:
                at_left = i * slots + t
            for u in range(per):
                found = cols_ref[safe, col_here * per + u]

                @pl.when((k >= 0) & (target >= 0) & (found == target))
                def _(u=u):
                    at = away * tile + lax.rem(safe, band_rows) * per + u
                    a = pltpu.make_async_copy(left_ref.at[at_left], left, sem.at[0])
                    b = pltpu.make_async_copy(panel_ref.at[at], right, sem.at[1])
                    a.start()
                    b.start()
                    a.wait()
                    b.wait()
                    acc[...] += jnp.dot(left[...], right[...], preferred_element_type=F32)

            return carry

        lax.fori_loop(0, slots, one_t, 0)
        out_ref[n] = acc[...]
        return carry

    lax.fori_loop(0, tile, one_out, 0)


def dense_step(rc, cols, left, panel, dims, mixed):
    _, band_rows, _, per = dims
    block = left.shape[1:]
    return pl.pallas_call(
        functools.partial(dense_body, dims=dims, mixed=mixed),
        out_shape=jax.ShapeDtypeStruct((band_rows * per, *block), F32),
        in_specs=[pl.BlockSpec(memory_space=pltpu.SMEM)] * 2
        + [pl.BlockSpec(memory_space=pl.ANY)] * 2,
        out_specs=pl.BlockSpec(memory_space=pltpu.VMEM),
        scratch_shapes=[
            pltpu.VMEM(block, BF16),
            pltpu.VMEM(block, BF16),
            pltpu.VMEM(block, F32),
            pltpu.SemaphoreType.DMA((2,)),
        ],
        name="dense_step",
    )(rc, cols, left, panel)


def dense(rc, cols, density, dims, sizes):
    _, band_rows, _, per = dims
    rows, slots, *block = density.shape
    row_size, col_size = sizes
    tile = lax.dynamic_slice_in_dim(density, rc[1] * per, per, 1)
    tile = tile.reshape(band_rows * per, *block)
    panel = spread(tile, "row", row_size, 2).reshape(-1, *block)
    square = dense_step(rc, cols, density.reshape(-1, *block), panel, dims, False)
    half = spread(square.astype(BF16), "col", col_size, 3).reshape(-1, *block)
    cube = dense_step(rc, cols, half, panel, dims, True)
    return (3.0 * square - 2.0 * cube).astype(BF16).reshape(rows, per, *block)


def local(density, cols, *, sizes):
    rows, slots, *block = density.shape
    row_size, col_size = sizes
    side = math.isqrt(row_size)
    per = slots // col_size
    width = cols.shape[0] // col_size
    dims = (side, rows, width, per)
    rc = jnp.stack([lax.axis_index("row"), lax.axis_index("col")]).astype(I32)
    band = density.reshape(rows * slots, *block)
    src1, src2, jobs, flag = make_plan(rc, cols, dims)
    near = (side - 1) * CAP1
    far = (side - 1) * CAP2
    packed = gather(src1, near, band)
    recv1, heard = ring(packed.reshape(side - 1, CAP1, *block), flag, side, col_size, 0)
    recv1 = recv1.reshape(near, *block)
    packed = gather(src2, far, recv1, band)
    (recv2,) = ring(packed.reshape(side - 1, CAP2, *block), None, side, col_size, 1)
    recv2 = recv2.reshape(far, *block)
    over = jnp.max(heard) + flag[0, 0] > 0
    return lax.cond(
        over,
        lambda: dense(rc, cols, density, dims, sizes),
        lambda: products(rc, jobs, band, recv1, recv2, rows, per),
    )


def solution(mesh):
    sizes = (mesh.shape["row"], mesh.shape["col"])
    return jax.shard_map(
        functools.partial(local, sizes=sizes),
        mesh=mesh,
        in_specs=(P("row", None, None, None), P()),
        out_specs=P("row", "col", None, None),
        check_vma=False,
    )
```

```python
import functools
import math

import jax
import jax.numpy as jnp
from jax import lax
from jax.experimental import pallas as pl
from jax.experimental.pallas import tpu as pltpu
from jax.sharding import PartitionSpec as P

F32 = jnp.float32
BF16 = jnp.bfloat16
I32 = jnp.int32
CAP1 = 40
CAP2 = 48
JOB = 1024
MESH = pl.DeviceIdType.MESH


def fdiv(x, n):
    return jnp.floor((x + 0.5) * (1.0 / n))


def mm(a, b, contract=((1,), (0,))):
    return lax.dot_general(
        a.astype(BF16), b.astype(BF16), (contract, ((), ())), preferred_element_type=F32
    )


NT = ((1,), (1,))


def ones_where(cond):
    return jnp.where(cond, 1.0, 0.0).astype(F32)


def plan_body(rc_ref, cols_ref, src1_ref, src2_ref, jobs_ref, flag_ref, own_ref, *, dims):
    side, band_rows, width, per = dims
    count, slots = cols_ref.shape
    row_here, col_here = rc_ref[0], rc_ref[1]
    odd = lax.rem(col_here, 2)
    hi_here = row_here // side
    lo_here = lax.rem(row_here, side)
    p_here = jnp.where(odd == 0, lo_here, hi_here)
    q_here = jnp.where(odd == 0, hi_here, lo_here)
    odd_f = odd.astype(F32)
    p_f, q_f = p_here.astype(F32), q_here.astype(F32)

    square = (count, count)
    row_at = lax.broadcasted_iota(I32, square, 0).astype(F32)
    lane_at = lax.broadcasted_iota(I32, square, 1).astype(F32)
    group = fdiv(lane_at, width)

    def coords(index):
        band = fdiv(index, band_rows)
        hi = fdiv(band, side)
        lo = band - side * hi
        p = odd_f * hi + (1.0 - odd_f) * lo
        q = odd_f * lo + (1.0 - odd_f) * hi
        p = p - p_f
        q = q - q_f
        return band, p + side * ones_where(p < 0.0), q + side * ones_where(q < 0.0)

    band, prel, qrel = coords(row_at)
    band_lane, _, qrel_lane = coords(lane_at)
    own_row = row_at - band_rows * band

    slot_row = lax.broadcasted_iota(I32, (slots, count), 0).astype(F32)
    slot_lane = lax.broadcasted_iota(I32, (slots, count), 1).astype(F32)
    cols = cols_ref[...].astype(F32)
    occupied = jnp.zeros(square, F32)
    slot = per * group
    for u in range(per):
        expand = ones_where(slot_row == per * fdiv(slot_lane, width) + u)
        hit = ones_where(mm(cols, expand) == lane_at)
        occupied = occupied + hit
        slot = slot + u * hit
    own_ref[...] = jnp.where(occupied > 0.0, slot, -1.0)

    in_group = ones_where(group == col_here.astype(F32))
    part = occupied * in_group
    shared = mm(part, part, NT)
    wanted = occupied * jnp.maximum(in_group, ones_where(shared > 0.0))
    identity = ones_where(row_at == lane_at)
    flipped = mm(identity, occupied, NT)
    wanted_b = wanted.astype(BF16)

    def needed_by(d, e):
        pd, qe = lax.rem(p_here + d, side), lax.rem(q_here + e, side)
        who = jnp.where(odd == 0, qe * side + pd, pd * side + qe).astype(F32)
        picked = flipped * ones_where(band_lane == who)
        return occupied * ones_where(mm(picked, wanted_b) > 0.0)

    before = ones_where(row_at < lane_at)
    in_band = ones_where((lane_at < row_at) & (band_lane == band))
    in_class = ones_where((lane_at < row_at) & (qrel_lane == qrel))
    everything = jnp.ones(square, BF16)

    def rank_of(need, earlier):
        return mm(need, before) + mm(mm(earlier, need), everything)

    class_row = lax.broadcasted_iota(I32, (8, count), 0).astype(F32)
    _, _, class_of = coords(lax.broadcasted_iota(I32, (8, count), 1).astype(F32))
    classes = ones_where(class_of == class_row)
    most1 = jnp.zeros((1, count), F32)
    most2 = jnp.zeros((8, 1), F32)
    union, direct = [], []
    for d in range(side):
        total = None
        for e in range(side):
            need = needed_by(d, e)
            sums = jnp.sum(mm(classes, need), axis=1, keepdims=True)
            sums = sums * ones_where(class_row[:, :1] != float(e))
            most2 = jnp.maximum(most2, sums)
            total = need if total is None else jnp.maximum(total, need)
            if d == 0:
                direct.append(need)
        union.append(total)
    rank1, rank2 = [], []
    for d in range(side):
        rank = rank_of(union[d], in_band)
        rank1.append(rank)
        used = (rank + 1.0) * union[d] * ones_where(prel != float(d))
        most1 = jnp.maximum(most1, jnp.max(used, axis=0, keepdims=True))
        rank2.append(rank_of(direct[d], in_class))
    over1 = jnp.max(most1, axis=1, keepdims=True) > float(CAP1)
    over2 = jnp.max(most2, axis=0, keepdims=True) > float(CAP2)
    over = jnp.where(over1 | over2, 1, 0).astype(I32)
    flag_ref[...] = jnp.broadcast_to(over, flag_ref.shape)

    def invert(rank, value_hi, value_lo, cap):
        rows = []
        value = 64.0 * value_hi + value_lo + 1.0
        for n in range(cap):
            rows.append(jnp.sum(jnp.where(rank == float(n + 1), value, 0.0), axis=0, keepdims=True))
        return jnp.concatenate(rows, axis=0)

    def to_lanes(stack):
        ones = jnp.ones((8, stack.shape[1]), F32)
        return lax.dot_general(
            ones, stack, (NT, ((), ())), preferred_element_type=F32, precision=lax.Precision.HIGHEST
        )

    sel_row = lax.broadcasted_iota(I32, (16, count), 0).astype(F32)
    sel_lane = lax.broadcasted_iota(I32, (16, count), 1).astype(F32)
    first = (row_here * band_rows).astype(F32)
    pick = ones_where((sel_lane == sel_row + first) & (sel_row < float(band_rows)))
    slot16 = mm(pick, slot)
    place = sel_row * slots + slot16
    zeros16 = jnp.zeros_like(place)
    stacks = []
    for d in range(1, side):
        rank = mm(pick, jnp.minimum((rank1[d] + 1.0) * union[d], 255.0))
        stacks.append(invert(rank, zeros16, place, CAP1))
    src1 = to_lanes(jnp.concatenate(stacks, axis=0))
    src1_ref[...] = src1.astype(I32)

    in_recv1 = (prel - 1.0) * CAP1 + jnp.minimum(rank1[0], CAP1 - 1.0)
    in_band_at = own_row * slots + slot
    after1 = jnp.where(prel == 0.0, (side - 1.0) * CAP1 + in_band_at, in_recv1)
    members = side * band_rows
    mem_row = lax.broadcasted_iota(I32, (members, count), 0).astype(F32)
    mem_lane = lax.broadcasted_iota(I32, (members, count), 1).astype(F32)
    mem_band, mem_p, mem_q = coords(mem_lane)
    pick = ones_where(
        (mem_q == 0.0) & (mem_p * band_rows + (mem_lane - band_rows * mem_band) == mem_row)
    )
    after_hi = fdiv(after1, 64)
    hi48 = mm(pick, after_hi)
    lo48 = mm(pick, after1 - 64.0 * after_hi)
    stacks = []
    for e in range(1, side):
        rank = mm(pick, jnp.minimum((rank2[e] + 1.0) * direct[e], 255.0))
        stacks.append(invert(rank, hi48, lo48, CAP2))
    src2 = to_lanes(jnp.concatenate(stacks, axis=0))
    src2_ref[...] = src2.astype(I32)

    held = band_rows * slots
    loc = jnp.where(
        prel + qrel == 0.0,
        in_band_at,
        jnp.where(
            qrel == 0.0,
            held + in_recv1,
            held + (side - 1.0) * CAP1 + (qrel - 1.0) * CAP2 + jnp.minimum(rank2[0], CAP2 - 1.0),
        ),
    )
    loc_hi = fdiv(loc, 64)
    loc_lo = (loc - 64.0 * loc_hi).astype(BF16)
    loc_hi = loc_hi.astype(BF16)
    occ_b = occupied.astype(BF16)
    small = (slots, count)
    t_at = lax.broadcasted_iota(I32, small, 0).astype(F32)
    wide_at = lax.broadcasted_iota(I32, (128, count), 0).astype(F32)
    pack = 4
    wide_i = fdiv(wide_at, 128 // pack)
    wide_t = wide_at - (128 // pack) * wide_i
    tri = ones_where(
        lax.broadcasted_iota(I32, (slots, slots), 1) < lax.broadcasted_iota(I32, (slots, slots), 0)
    )
    t_out = lax.broadcasted_iota(I32, (slots, 128), 0).astype(F32)
    wanted_rows = mm(jnp.where(sel_row + first == sel_lane, 1.0, 0.0), wanted)
    for g in range(band_rows // pack):
        exists = jnp.zeros((slots, 128), F32)
        at_hi = jnp.zeros((slots, 128), F32)
        at_lo = jnp.zeros((slots, 128), F32)
        for ii in range(pack):
            i = g * pack + ii
            line = own_ref[pl.ds(row_here * band_rows + i, 1), :]
            left = ones_where(t_at == line).astype(BF16)
            right = ones_where((wide_i == float(ii)) & (wide_t == line))
            right = (right * wanted_rows[i : i + 1, :]).astype(BF16)
            exists = exists + mm(mm(left, occ_b), right, NT)
            at_hi = at_hi + mm(mm(left, loc_hi), right, NT)
            at_lo = at_lo + mm(mm(left, loc_lo), right, NT)
        rank = jnp.where(exists > 0.0, mm(tri, exists), -1.0)
        code = t_out * JOB + at_hi * 64.0 + at_lo
        rows = []
        for n in range(slots):
            rows.append(jnp.sum(jnp.where(rank == float(n), code, 0.0), axis=0, keepdims=True))
        rows.append(jnp.sum(exists, axis=0, keepdims=True))
        flags = jnp.zeros((1, 128), F32)
        for ii in range(pack):
            i = g * pack + ii
            line = own_ref[pl.ds(row_here * band_rows + i, 1), :]
            right = ones_where((wide_i == float(ii)) & (wide_t == line)).astype(BF16)
            mark = jnp.broadcast_to(wanted_rows[i : i + 1, :], (8, count))
            flags = flags + mm(mark, right, NT)[:1]
        rows.append(flags)
        rows.append(jnp.zeros((32 - slots - 2, 128), F32))
        jobs_ref[g] = jnp.concatenate(rows, axis=0).astype(I32)


def make_plan(rc, cols, dims):
    side, band_rows, _, _ = dims
    count = cols.shape[0]
    groups = band_rows // 4
    return pl.pallas_call(
        functools.partial(plan_body, dims=dims),
        out_shape=(
            jax.ShapeDtypeStruct((8, (side - 1) * CAP1), I32),
            jax.ShapeDtypeStruct((8, (side - 1) * CAP2), I32),
            jax.ShapeDtypeStruct((groups, 32, 128), I32),
            jax.ShapeDtypeStruct((8, 128), I32),
        ),
        in_specs=[
            pl.BlockSpec(memory_space=pltpu.SMEM),
            pl.BlockSpec(memory_space=pltpu.VMEM),
        ],
        out_specs=[pl.BlockSpec(memory_space=pltpu.VMEM)] * 4,
        scratch_shapes=[pltpu.VMEM((count, count), F32)],
        name="plan",
    )(rc, cols)


def gather_body(index_ref, *refs, sizes):
    sources, out_ref, sem = refs[: len(sizes)], refs[len(sizes)], refs[-1]
    total = out_ref.shape[0]

    def issue(n, count):
        at = index_ref[0, n] - 1
        start = 0
        for ref, size in zip(sources, sizes):
            inside = (at >= start) & (at < start + size)

            @pl.when(inside)
            def _(ref=ref, start=start):
                pltpu.make_async_copy(ref.at[at - start], out_ref.at[n], sem).start()

            start += size
        return count + jnp.where(at >= 0, 1, 0)

    count = lax.fori_loop(0, total, issue, jnp.zeros((), I32), unroll=4)

    def settle(n, carry):
        pltpu.make_async_copy(out_ref.at[0], out_ref.at[0], sem).wait()
        return carry

    lax.fori_loop(0, count, settle, 0)


def gather(index, total, *sources):
    block = sources[0].shape[1:]
    return pl.pallas_call(
        functools.partial(gather_body, sizes=tuple(s.shape[0] for s in sources)),
        out_shape=jax.ShapeDtypeStruct((total, *block), sources[0].dtype),
        in_specs=[pl.BlockSpec(memory_space=pltpu.SMEM)]
        + [pl.BlockSpec(memory_space=pl.ANY)] * len(sources),
        out_specs=pl.BlockSpec(memory_space=pltpu.VMEM),
        scratch_shapes=[pltpu.SemaphoreType.DMA],
        name="gather",
    )(index, *sources)


def ring_body(*refs, side, cols, stage, flags):
    if flags:
        send_ref, flag_ref, recv_ref, heard_ref = refs[:4]
    else:
        send_ref, recv_ref = refs[:2]
    relay_up, relay_down, send_sem, recv_sem = refs[-4:]
    row, col = lax.axis_index("row"), lax.axis_index("col")
    hi, lo = row // side, lax.rem(row, side)
    low_axis = lax.rem(col + stage, 2)

    def along(d):
        by_lo = hi * side + lax.rem(lo + d, side)
        by_hi = lax.rem(hi + d, side) * side + lo
        return (by_lo * (1 - low_axis) + by_hi * low_axis, col)

    right, left = along(1), along(side - 1)
    peers = [(row, lax.rem(col + k, cols)) for k in range(1, cols)] if flags else []
    barrier = pltpu.get_barrier_semaphore()
    for peer in [right, left, *peers]:
        pl.semaphore_signal(barrier, inc=1, device_id=peer, device_id_type=MESH)
    pl.semaphore_wait(barrier, 2 + len(peers))

    half = send_ref.shape[1] // 2
    lower, upper = pl.ds(0, half), pl.ds(half, half)

    def copy(n, src, dst, peer):
        return pltpu.make_async_remote_copy(
            src_ref=src,
            dst_ref=dst,
            send_sem=send_sem.at[n],
            recv_sem=recv_sem.at[n],
            device_id=peer,
            device_id_type=MESH,
        )

    far_up = copy(0, send_ref.at[1, lower], relay_up, right)
    far_down = copy(1, send_ref.at[1, upper], relay_down, left)
    near_up = copy(2, send_ref.at[0], recv_ref.at[2], right)
    near_down = copy(3, send_ref.at[2], recv_ref.at[0], left)
    next_up = copy(4, relay_up, recv_ref.at[1, lower], right)
    next_down = copy(5, relay_down, recv_ref.at[1, upper], left)
    told = [copy(6 + k, flag_ref, heard_ref.at[k], peer) for k, peer in enumerate(peers)]
    far_up.start()
    far_down.start()
    near_up.start()
    near_down.start()
    for one in told:
        one.start()
    far_up.wait_recv()
    next_up.start()
    far_down.wait_recv()
    next_down.start()
    far_up.wait_send()
    far_down.wait_send()
    for one in told:
        one.wait()
    near_up.wait()
    near_down.wait()
    next_up.wait()
    next_down.wait()


def ring(send, flag, side, cols, stage):
    three, cap, *block = send.shape
    flags = flag is not None
    copies = 6 + (cols - 1 if flags else 0)
    out_shape = [jax.ShapeDtypeStruct(send.shape, send.dtype)]
    if flags:
        out_shape.append(jax.ShapeDtypeStruct((cols - 1, *flag.shape), flag.dtype))
    return pl.pallas_call(
        functools.partial(ring_body, side=side, cols=cols, stage=stage, flags=flags),
        out_shape=out_shape,
        in_specs=[pl.BlockSpec(memory_space=pl.ANY)] * (2 if flags else 1),
        out_specs=[pl.BlockSpec(memory_space=pl.ANY)] * len(out_shape),
        scratch_shapes=[
            pltpu.VMEM((cap // 2, *block), send.dtype),
            pltpu.VMEM((cap // 2, *block), send.dtype),
            pltpu.SemaphoreType.DMA((copies,)),
            pltpu.SemaphoreType.DMA((copies,)),
        ],
        compiler_params=pltpu.CompilerParams(collective_id=stage, has_side_effects=True),
        name="ring",
    )(*([send, flag] if flags else [send]))


def products_body(
    rc_ref, jobs_ref, band_ref, recv1_ref, recv2_ref, out_ref, held, half, square, cube, todo, extra, sem, *, per
):
    n_band, n1, n2 = band_ref.shape[0], recv1_ref.shape[0], recv2_ref.shape[0]
    copies = [
        pltpu.make_async_copy(band_ref, held.at[pl.ds(0, n_band)], sem.at[0]),
        pltpu.make_async_copy(recv1_ref, held.at[pl.ds(n_band, n1)], sem.at[1]),
        pltpu.make_async_copy(recv2_ref, held.at[pl.ds(n_band + n1, n2)], sem.at[2]),
    ]
    for one in copies:
        one.start()
    rows = out_ref.shape[0]
    tile = rows * per
    slots = n_band // rows
    block = out_ref.shape[2:]
    blank = n_band + n1 + n2
    first_own = rc_ref[1] * per
    held[blank] = jnp.zeros(block, BF16)
    half[n_band] = jnp.zeros(block, BF16)

    def listed(i, t, number, own_at, count, more, left_blank):
        g, lane = i // 4, lax.rem(i, 4) * 32 + t
        n = jobs_ref[g, slots, lane]
        todo[0, count] = number
        todo[1, count] = own_at
        for q in range(2):
            code = jobs_ref[g, q, lane]
            there = n > q
            todo[2 + 2 * q, count] = jnp.where(there, i * slots + code // JOB, left_blank)
            todo[3 + 2 * q, count] = jnp.where(there, lax.rem(code, JOB), blank)
        extra[0, more] = number
        extra[1, more] = own_at
        extra[2, more] = i
        extra[3, more] = t
        return count + 1, more + jnp.where(n > 2, 1, 0)

    def plan_row(i, carry):
        def plan_one(t, carry):
            count, more = carry
            g, lane = i // 4, lax.rem(i, 4) * 32 + t
            s = t - first_own
            own = (s >= 0) & (s < per)
            wanted = (jobs_ref[g, slots + 1, lane] > 0) | own
            own_at = jnp.where(own, i * per + s, tile)
            after, extra_after = listed(i, t, i * slots + t, own_at, count, more, blank)
            return jnp.where(wanted, after, count), jnp.where(wanted, extra_after, more)

        return lax.fori_loop(0, slots, plan_one, carry)

    zero = jnp.zeros((), I32)
    count, more = lax.fori_loop(0, rows, plan_row, (zero, zero))

    def pad(k, carry):
        todo[0, count + k] = n_band
        todo[1, count + k] = tile
        for q in range(2, 6):
            todo[q, count + k] = blank
        return carry

    lax.fori_loop(0, 3, pad, 0)
    for one in copies:
        one.wait()

    def pair(left, m):
        a = jnp.concatenate([left[todo[2, m]], left[todo[4, m]]], axis=1)
        b = jnp.concatenate([held[todo[3, m]], held[todo[5, m]]], axis=0)
        return jnp.dot(a, b, preferred_element_type=F32)

    def rest(left, i, t, acc):
        g, lane = i // 4, lax.rem(i, 4) * 32 + t

        def step(q, acc):
            code = jobs_ref[g, q, lane]
            a = left[i * slots + code // JOB]
            return acc + jnp.dot(a, held[lax.rem(code, JOB)], preferred_element_type=F32)

        return lax.fori_loop(2, jobs_ref[g, slots, lane], step, acc)

    def four(m4, carry):
        sums = [pair(held, m4 * 4 + k) for k in range(4)]
        for k in range(4):
            half[todo[0, m4 * 4 + k]] = sums[k].astype(BF16)
        for k in range(4):
            square[todo[1, m4 * 4 + k]] = sums[k]
        return carry

    lax.fori_loop(0, (count + 3) // 4, four, 0)

    def late(m, carry):
        i, t = extra[2, m], extra[3, m]
        code0, code1 = jobs_ref[i // 4, 0, lax.rem(i, 4) * 32 + t], jobs_ref[i // 4, 1, lax.rem(i, 4) * 32 + t]
        acc = jnp.dot(held[i * slots + code0 // JOB], held[lax.rem(code0, JOB)], preferred_element_type=F32)
        acc = acc + jnp.dot(
            held[i * slots + code1 // JOB], held[lax.rem(code1, JOB)], preferred_element_type=F32
        )
        acc = rest(held, i, t, acc)
        half[extra[0, m]] = acc.astype(BF16)
        square[extra[1, m]] = acc
        return carry

    lax.fori_loop(0, more, late, 0)

    def plan_cube(n, more):
        i, s = n // per, lax.rem(n, per)
        _, after = listed(i, first_own + s, n, n, n, more, n_band)
        return after

    more = lax.fori_loop(0, tile, plan_cube, zero)

    def four_cubes(m4, carry):
        sums = [pair(half, m4 * 4 + k) for k in range(4)]
        for k in range(4):
            cube[m4 * 4 + k] = sums[k]
        return carry

    lax.fori_loop(0, tile // 4, four_cubes, 0)

    def late_cube(m, carry):
        n = extra[0, m]
        cube[n] = rest(half, extra[2, m], extra[3, m], cube[n])
        return carry

    lax.fori_loop(0, more, late_cube, 0)
    for i in range(rows):
        for s in range(per):
            n = i * per + s
            out_ref[i, s] = (3.0 * square[n] - 2.0 * cube[n]).astype(BF16)


def products(rc, jobs, band, recv1, recv2, rows, per):
    block = band.shape[1:]
    blocks = band.shape[0] + recv1.shape[0] + recv2.shape[0]
    lists = band.shape[0] + 8
    return pl.pallas_call(
        functools.partial(products_body, per=per),
        out_shape=jax.ShapeDtypeStruct((rows, per, *block), BF16),
        in_specs=[pl.BlockSpec(memory_space=pltpu.SMEM)] * 2
        + [pl.BlockSpec(memory_space=pl.ANY)] * 3,
        out_specs=pl.BlockSpec(memory_space=pltpu.VMEM),
        scratch_shapes=[
            pltpu.VMEM((blocks + 1, *block), BF16),
            pltpu.VMEM((band.shape[0] + 1, *block), BF16),
            pltpu.VMEM((rows * per + 1, *block), F32),
            pltpu.VMEM((rows * per, *block), F32),
            pltpu.SMEM((6, lists), I32),
            pltpu.SMEM((4, lists), I32),
            pltpu.SemaphoreType.DMA((3,)),
        ],
        compiler_params=pltpu.CompilerParams(vmem_limit_bytes=60 * 1024 * 1024),
        name="products",
    )(rc, jobs, band, recv1, recv2)


def spread_body(x_ref, out_ref, send_sem, recv_sem, *, axis, size):
    row, col = lax.axis_index("row"), lax.axis_index("col")

    def peer(k):
        if axis == "row":
            return (lax.rem(row + k, size), col)
        return (row, lax.rem(col + k, size))

    barrier = pltpu.get_barrier_semaphore()
    for k in range(1, size):
        pl.semaphore_signal(barrier, inc=1, device_id=peer(k), device_id_type=MESH)
    pl.semaphore_wait(barrier, size - 1)
    copies = []
    for k in range(1, size):
        one = pltpu.make_async_remote_copy(
            src_ref=x_ref,
            dst_ref=out_ref.at[k - 1],
            send_sem=send_sem.at[k - 1],
            recv_sem=recv_sem.at[k - 1],
            device_id=peer(k),
            device_id_type=MESH,
        )
        one.start()
        copies.append(one)
    for one in copies:
        one.wait()


def spread(x, axis, size, collective_id):
    others = pl.pallas_call(
        functools.partial(spread_body, axis=axis, size=size),
        out_shape=jax.ShapeDtypeStruct((size - 1, *x.shape), x.dtype),
        in_specs=[pl.BlockSpec(memory_space=pl.ANY)],
        out_specs=pl.BlockSpec(memory_space=pl.ANY),
        scratch_shapes=[pltpu.SemaphoreType.DMA((size - 1,)), pltpu.SemaphoreType.DMA((size - 1,))],
        compiler_params=pltpu.CompilerParams(collective_id=collective_id, has_side_effects=True),
        name="spread",
    )(x)
    return jnp.concatenate([x[None], others], axis=0)


def dense_body(rc_ref, cols_ref, left_ref, panel_ref, out_ref, left, right, acc, sem, *, dims, mixed):
    side, band_rows, _, per = dims
    slots = cols_ref.shape[1]
    row_here, col_here = rc_ref[0], rc_ref[1]
    tile = band_rows * per
    row_count, col_count = side * side, slots // per

    def one_out(n, carry):
        i, s = n // per, lax.rem(n, per)
        target = cols_ref[row_here * band_rows + i, col_here * per + s]
        acc[...] = jnp.zeros_like(acc)

        def one_t(t, carry):
            k = cols_ref[row_here * band_rows + i, t]
            safe = jnp.maximum(k, 0)
            away = lax.rem(row_here - safe // band_rows + row_count, row_count)
            if mixed:
                back = lax.rem(col_here - t // per + col_count, col_count)
                at_left = back * tile + i * per + lax.rem(t, per)
            else:
                at_left = i * slots + t
            for u in range(per):
                found = cols_ref[safe, col_here * per + u]

                @pl.when((k >= 0) & (target >= 0) & (found == target))
                def _(u=u):
                    at = away * tile + lax.rem(safe, band_rows) * per + u
                    a = pltpu.make_async_copy(left_ref.at[at_left], left, sem.at[0])
                    b = pltpu.make_async_copy(panel_ref.at[at], right, sem.at[1])
                    a.start()
                    b.start()
                    a.wait()
                    b.wait()
                    acc[...] += jnp.dot(left[...], right[...], preferred_element_type=F32)

            return carry

        lax.fori_loop(0, slots, one_t, 0)
        out_ref[n] = acc[...]
        return carry

    lax.fori_loop(0, tile, one_out, 0)


def dense_step(rc, cols, left, panel, dims, mixed):
    _, band_rows, _, per = dims
    block = left.shape[1:]
    return pl.pallas_call(
        functools.partial(dense_body, dims=dims, mixed=mixed),
        out_shape=jax.ShapeDtypeStruct((band_rows * per, *block), F32),
        in_specs=[pl.BlockSpec(memory_space=pltpu.SMEM)] * 2
        + [pl.BlockSpec(memory_space=pl.ANY)] * 2,
        out_specs=pl.BlockSpec(memory_space=pltpu.VMEM),
        scratch_shapes=[
            pltpu.VMEM(block, BF16),
            pltpu.VMEM(block, BF16),
            pltpu.VMEM(block, F32),
            pltpu.SemaphoreType.DMA((2,)),
        ],
        name="dense_step",
    )(rc, cols, left, panel)


def dense(rc, cols, density, dims, sizes):
    _, band_rows, _, per = dims
    rows, slots, *block = density.shape
    row_size, col_size = sizes
    tile = lax.dynamic_slice_in_dim(density, rc[1] * per, per, 1)
    tile = tile.reshape(band_rows * per, *block)
    panel = spread(tile, "row", row_size, 2).reshape(-1, *block)
    square = dense_step(rc, cols, density.reshape(-1, *block), panel, dims, False)
    half = spread(square.astype(BF16), "col", col_size, 3).reshape(-1, *block)
    cube = dense_step(rc, cols, half, panel, dims, True)
    return (3.0 * square - 2.0 * cube).astype(BF16).reshape(rows, per, *block)


def local(density, cols, *, sizes):
    rows, slots, *block = density.shape
    row_size, col_size = sizes
    side = math.isqrt(row_size)
    per = slots // col_size
    width = cols.shape[0] // col_size
    dims = (side, rows, width, per)
    rc = jnp.stack([lax.axis_index("row"), lax.axis_index("col")]).astype(I32)
    band = density.reshape(rows * slots, *block)
    src1, src2, jobs, flag = make_plan(rc, cols, dims)
    near = (side - 1) * CAP1
    far = (side - 1) * CAP2
    packed = gather(src1, near, band)
    recv1, heard = ring(packed.reshape(side - 1, CAP1, *block), flag, side, col_size, 0)
    recv1 = recv1.reshape(near, *block)
    packed = gather(src2, far, recv1, band)
    (recv2,) = ring(packed.reshape(side - 1, CAP2, *block), None, side, col_size, 1)
    recv2 = recv2.reshape(far, *block)
    over = jnp.max(heard) + flag[0, 0] > 0
    return lax.cond(
        over,
        lambda: dense(rc, cols, density, dims, sizes),
        lambda: products(rc, jobs, band, recv1, recv2, rows, per),
    )


def solution(mesh):
    sizes = (mesh.shape["row"], mesh.shape["col"])
    return jax.shard_map(
        functools.partial(local, sizes=sizes),
        mesh=mesh,
        in_specs=(P("row", None, None, None), P()),
        out_specs=P("row", "col", None, None),
        check_vma=False,
    )
```

```python
import functools
import math

import jax
import jax.numpy as jnp
from jax import lax
from jax.experimental import pallas as pl
from jax.experimental.pallas import tpu as pltpu
from jax.sharding import PartitionSpec as P

F32 = jnp.float32
BF16 = jnp.bfloat16
I32 = jnp.int32
CAP1 = 40
CAP2 = 48
JOB = 1024
LEVELS = 3
MESH = pl.DeviceIdType.MESH


def fdiv(x, n):
    return jnp.floor((x + 0.5) * (1.0 / n))


def mm(a, b, contract=((1,), (0,))):
    return lax.dot_general(
        a.astype(BF16), b.astype(BF16), (contract, ((), ())), preferred_element_type=F32
    )


NT = ((1,), (1,))


def ones_where(cond):
    return jnp.where(cond, 1.0, 0.0).astype(F32)


def plan_body(rc_ref, cols_ref, src1_ref, src2_ref, jobs_ref, todo_ref, flag_ref, own_ref, *, dims):
    side, band_rows, width, per = dims
    count, slots = cols_ref.shape
    row_here, col_here = rc_ref[0], rc_ref[1]
    odd = lax.rem(col_here, 2)
    hi_here = row_here // side
    lo_here = lax.rem(row_here, side)
    p_here = jnp.where(odd == 0, lo_here, hi_here)
    q_here = jnp.where(odd == 0, hi_here, lo_here)
    odd_f = odd.astype(F32)
    p_f, q_f = p_here.astype(F32), q_here.astype(F32)

    square = (count, count)
    row_at = lax.broadcasted_iota(I32, square, 0).astype(F32)
    lane_at = lax.broadcasted_iota(I32, square, 1).astype(F32)
    group = fdiv(lane_at, width)

    def coords(index):
        band = fdiv(index, band_rows)
        hi = fdiv(band, side)
        lo = band - side * hi
        p = odd_f * hi + (1.0 - odd_f) * lo
        q = odd_f * lo + (1.0 - odd_f) * hi
        p = p - p_f
        q = q - q_f
        return band, p + side * ones_where(p < 0.0), q + side * ones_where(q < 0.0)

    band, prel, qrel = coords(row_at)
    band_lane, _, qrel_lane = coords(lane_at)
    own_row = row_at - band_rows * band

    slot_row = lax.broadcasted_iota(I32, (slots, count), 0).astype(F32)
    slot_lane = lax.broadcasted_iota(I32, (slots, count), 1).astype(F32)
    cols = cols_ref[...].astype(F32)
    occupied = jnp.zeros(square, F32)
    slot = per * group
    for u in range(per):
        expand = ones_where(slot_row == per * fdiv(slot_lane, width) + u)
        hit = ones_where(mm(cols, expand) == lane_at)
        occupied = occupied + hit
        slot = slot + u * hit
    own_ref[...] = jnp.where(occupied > 0.0, slot, -1.0)

    in_group = ones_where(group == col_here.astype(F32))
    part = occupied * in_group
    shared = mm(part, part, NT)
    wanted = occupied * jnp.maximum(in_group, ones_where(shared > 0.0))
    identity = ones_where(row_at == lane_at)
    flipped = mm(identity, occupied, NT)
    wanted_b = wanted.astype(BF16)

    def needed_by(d, e):
        pd, qe = lax.rem(p_here + d, side), lax.rem(q_here + e, side)
        who = jnp.where(odd == 0, qe * side + pd, pd * side + qe).astype(F32)
        picked = flipped * ones_where(band_lane == who)
        return occupied * ones_where(mm(picked, wanted_b) > 0.0)

    before = ones_where(row_at < lane_at)
    in_band = ones_where((lane_at < row_at) & (band_lane == band))
    in_class = ones_where((lane_at < row_at) & (qrel_lane == qrel))
    everything = jnp.ones(square, BF16)

    def rank_of(need, earlier):
        return mm(need, before) + mm(mm(earlier, need), everything)

    class_row = lax.broadcasted_iota(I32, (8, count), 0).astype(F32)
    _, _, class_of = coords(lax.broadcasted_iota(I32, (8, count), 1).astype(F32))
    classes = ones_where(class_of == class_row)
    most1 = jnp.zeros((1, count), F32)
    most2 = jnp.zeros((8, 1), F32)
    union, direct = [], []
    for d in range(side):
        total = None
        for e in range(side):
            need = needed_by(d, e)
            sums = jnp.sum(mm(classes, need), axis=1, keepdims=True)
            sums = sums * ones_where(class_row[:, :1] != float(e))
            most2 = jnp.maximum(most2, sums)
            total = need if total is None else jnp.maximum(total, need)
            if d == 0:
                direct.append(need)
        union.append(total)
    rank1, rank2 = [], []
    for d in range(side):
        rank = rank_of(union[d], in_band)
        rank1.append(rank)
        used = (rank + 1.0) * union[d] * ones_where(prel != float(d))
        most1 = jnp.maximum(most1, jnp.max(used, axis=0, keepdims=True))
        rank2.append(rank_of(direct[d], in_class))
    over1 = jnp.max(most1, axis=1, keepdims=True) > float(CAP1)
    over2 = jnp.max(most2, axis=0, keepdims=True) > float(CAP2)
    over = jnp.where(over1 | over2, 1, 0).astype(I32)
    flag_ref[...] = jnp.broadcast_to(over, flag_ref.shape)

    def invert(rank, value_hi, value_lo, cap):
        rows = []
        value = 64.0 * value_hi + value_lo + 1.0
        for n in range(cap):
            rows.append(jnp.sum(jnp.where(rank == float(n + 1), value, 0.0), axis=0, keepdims=True))
        return jnp.concatenate(rows, axis=0)

    def to_lanes(stack):
        ones = jnp.ones((8, stack.shape[1]), F32)
        return lax.dot_general(
            ones, stack, (NT, ((), ())), preferred_element_type=F32, precision=lax.Precision.HIGHEST
        )

    sel_row = lax.broadcasted_iota(I32, (16, count), 0).astype(F32)
    sel_lane = lax.broadcasted_iota(I32, (16, count), 1).astype(F32)
    first = (row_here * band_rows).astype(F32)
    pick = ones_where((sel_lane == sel_row + first) & (sel_row < float(band_rows)))
    slot16 = mm(pick, slot)
    place = sel_row * slots + slot16
    zeros16 = jnp.zeros_like(place)
    stacks = []
    for d in range(1, side):
        rank = mm(pick, jnp.minimum((rank1[d] + 1.0) * union[d], 255.0))
        stacks.append(invert(rank, zeros16, place, CAP1))
    src1 = to_lanes(jnp.concatenate(stacks, axis=0))
    src1_ref[...] = src1.astype(I32)

    in_recv1 = (prel - 1.0) * CAP1 + jnp.minimum(rank1[0], CAP1 - 1.0)
    in_band_at = own_row * slots + slot
    after1 = jnp.where(prel == 0.0, (side - 1.0) * CAP1 + in_band_at, in_recv1)
    members = side * band_rows
    mem_row = lax.broadcasted_iota(I32, (members, count), 0).astype(F32)
    mem_lane = lax.broadcasted_iota(I32, (members, count), 1).astype(F32)
    mem_band, mem_p, mem_q = coords(mem_lane)
    pick = ones_where(
        (mem_q == 0.0) & (mem_p * band_rows + (mem_lane - band_rows * mem_band) == mem_row)
    )
    after_hi = fdiv(after1, 64)
    hi48 = mm(pick, after_hi)
    lo48 = mm(pick, after1 - 64.0 * after_hi)
    stacks = []
    for e in range(1, side):
        rank = mm(pick, jnp.minimum((rank2[e] + 1.0) * direct[e], 255.0))
        stacks.append(invert(rank, hi48, lo48, CAP2))
    src2 = to_lanes(jnp.concatenate(stacks, axis=0))
    src2_ref[...] = src2.astype(I32)

    held = band_rows * slots
    loc = jnp.where(
        prel + qrel == 0.0,
        in_band_at,
        jnp.where(
            qrel == 0.0,
            held + 1.0 + in_recv1,
            held + 1.0 + (side - 1.0) * CAP1 + (qrel - 1.0) * CAP2 + jnp.minimum(rank2[0], CAP2 - 1.0),
        ),
    )
    loc_hi = fdiv(loc, 64)
    loc_lo = (loc - 64.0 * loc_hi).astype(BF16)
    loc_hi = loc_hi.astype(BF16)
    occ_b = occupied.astype(BF16)
    small = (slots, count)
    t_at = lax.broadcasted_iota(I32, small, 0).astype(F32)
    wide_at = lax.broadcasted_iota(I32, (128, count), 0).astype(F32)
    pack = 4
    wide_i = fdiv(wide_at, 128 // pack)
    wide_t = wide_at - (128 // pack) * wide_i
    tri = ones_where(
        lax.broadcasted_iota(I32, (slots, slots), 1) < lax.broadcasted_iota(I32, (slots, slots), 0)
    )
    t_out = lax.broadcasted_iota(I32, (slots, 128), 0).astype(F32)
    wanted_rows = mm(jnp.where(sel_row + first == sel_lane, 1.0, 0.0), wanted)
    parts = []
    for g in range(band_rows // pack):
        exists = jnp.zeros((slots, 128), F32)
        at_hi = jnp.zeros((slots, 128), F32)
        at_lo = jnp.zeros((slots, 128), F32)
        flags = jnp.zeros((1, 128), F32)
        for ii in range(pack):
            i = g * pack + ii
            line = own_ref[pl.ds(row_here * band_rows + i, 1), :]
            left = ones_where(t_at == line).astype(BF16)
            right = ones_where((wide_i == float(ii)) & (wide_t == line))
            right = (right * wanted_rows[i : i + 1, :]).astype(BF16)
            exists = exists + mm(mm(left, occ_b), right, NT)
            at_hi = at_hi + mm(mm(left, loc_hi), right, NT)
            at_lo = at_lo + mm(mm(left, loc_lo), right, NT)
            flags = flags + mm(jnp.ones((8, count), BF16), right, NT)[:1]
        rank = jnp.where(exists > 0.0, mm(tri, exists), -1.0)
        code = t_out * JOB + at_hi * 64.0 + at_lo
        rows = []
        for n in range(slots):
            rows.append(jnp.sum(jnp.where(rank == float(n), code, 0.0), axis=0, keepdims=True))
        rows.append(jnp.sum(exists, axis=0, keepdims=True))
        rows.append(flags)
        parts.append(rows)
        spare = jnp.zeros((32 - slots - 2, 128), F32)
        jobs_ref[g] = jnp.concatenate([*rows, spare], axis=0).astype(I32)

    lanes = 128 * len(parts)

    def whole(n):
        return jnp.concatenate([rows[n] for rows in parts], axis=1)

    at = lax.broadcasted_iota(I32, (1, lanes), 1).astype(F32)
    i_at = fdiv(at, 128 // pack)
    t_of = at - (128 // pack) * i_at
    mine = t_of - per * col_here.astype(F32)
    own = ones_where((mine >= 0.0) & (mine < per))
    number_of = i_at * slots + t_of
    own_at = i_at * per + mine
    n_of = whole(slots)
    needed = jnp.maximum(whole(slots + 1), own)
    upper = ones_where(
        lax.broadcasted_iota(I32, (lanes, lanes), 0) < lax.broadcasted_iota(I32, (lanes, lanes), 1)
    ).astype(BF16)
    place_at = lax.broadcasted_iota(I32, (lanes, lanes), 0).astype(F32)
    slot_here = lax.broadcasted_iota(I32, (1, lanes), 1).astype(F32)
    most = jnp.max(n_of, axis=1, keepdims=True)

    def split(value):
        high = fdiv(value, 64)
        return [high, value - 64.0 * high]

    blank = float(held)
    for level in range(LEVELS):
        codes = [whole(2 * level + q) for q in range(2)]
        fields = split(number_of) + split(own_at * own)
        for q in range(2):
            there = n_of > float(2 * level + q)
            t_left = fdiv(codes[q], JOB)
            fields += split(jnp.where(there, i_at * slots + t_left, blank))
            fields += split(jnp.where(there, codes[q] - JOB * t_left, blank))
        table = jnp.concatenate(fields + [jnp.zeros((4, lanes), F32)], axis=0)
        for kind in range(2):
            mask = own if kind else needed
            if level > 0:
                mask = mask * ones_where(n_of > float(2 * level))
            rank = mm(jnp.broadcast_to(mask, (8, lanes)), upper)[:1]
            rank = jnp.where(mask > 0.0, rank, -1.0)
            packed = mm(table, ones_where(place_at == rank), NT)
            total = jnp.sum(mask, axis=1, keepdims=True)
            valid = slot_here < total
            spare = [blank, float(band_rows * per), blank, blank, blank, blank]
            rows = []
            for f in range(6):
                value = packed[2 * f : 2 * f + 1] * 64.0 + packed[2 * f + 1 : 2 * f + 2]
                rows.append(jnp.where(valid, value, spare[f]))
            rows.append(jnp.broadcast_to(total, (1, lanes)))
            rows.append(jnp.broadcast_to(most, (1, lanes)))
            todo_ref[2 * level + kind] = jnp.concatenate(rows, axis=0).astype(I32)


def make_plan(rc, cols, dims):
    side, band_rows, _, _ = dims
    count = cols.shape[0]
    groups = band_rows // 4
    return pl.pallas_call(
        functools.partial(plan_body, dims=dims),
        out_shape=(
            jax.ShapeDtypeStruct((8, (side - 1) * CAP1), I32),
            jax.ShapeDtypeStruct((8, (side - 1) * CAP2), I32),
            jax.ShapeDtypeStruct((groups, 32, 128), I32),
            jax.ShapeDtypeStruct((2 * LEVELS, 8, 128 * groups), I32),
            jax.ShapeDtypeStruct((8, 128), I32),
        ),
        in_specs=[
            pl.BlockSpec(memory_space=pltpu.SMEM),
            pl.BlockSpec(memory_space=pltpu.VMEM),
        ],
        out_specs=[pl.BlockSpec(memory_space=pltpu.VMEM)] * 5,
        scratch_shapes=[pltpu.VMEM((count, count), F32)],
        name="plan",
    )(rc, cols)


def gather_body(index_ref, *refs, sizes):
    sources, out_ref, sem = refs[: len(sizes)], refs[len(sizes)], refs[-1]
    total = out_ref.shape[0]

    def issue(n, count):
        at = index_ref[0, n] - 1
        start = 0
        for ref, size in zip(sources, sizes):
            inside = (at >= start) & (at < start + size)

            @pl.when(inside)
            def _(ref=ref, start=start):
                pltpu.make_async_copy(ref.at[at - start], out_ref.at[n], sem).start()

            start += size
        return count + jnp.where(at >= 0, 1, 0)

    count = lax.fori_loop(0, total, issue, jnp.zeros((), I32), unroll=4)

    def settle(n, carry):
        pltpu.make_async_copy(out_ref.at[0], out_ref.at[0], sem).wait()
        return carry

    lax.fori_loop(0, count, settle, 0)


def gather(index, total, *sources):
    block = sources[0].shape[1:]
    return pl.pallas_call(
        functools.partial(gather_body, sizes=tuple(s.shape[0] for s in sources)),
        out_shape=jax.ShapeDtypeStruct((total, *block), sources[0].dtype),
        in_specs=[pl.BlockSpec(memory_space=pltpu.SMEM)]
        + [pl.BlockSpec(memory_space=pl.ANY)] * len(sources),
        out_specs=pl.BlockSpec(memory_space=pltpu.VMEM),
        scratch_shapes=[pltpu.SemaphoreType.DMA],
        name="gather",
    )(index, *sources)


def ring_body(*refs, side, cols, stage, flags):
    if flags:
        send_ref, flag_ref, recv_ref, heard_ref = refs[:4]
    else:
        send_ref, recv_ref = refs[:2]
    relay_up, relay_down, send_sem, recv_sem = refs[-4:]
    row, col = lax.axis_index("row"), lax.axis_index("col")
    hi, lo = row // side, lax.rem(row, side)
    low_axis = lax.rem(col + stage, 2)

    def along(d):
        by_lo = hi * side + lax.rem(lo + d, side)
        by_hi = lax.rem(hi + d, side) * side + lo
        return (by_lo * (1 - low_axis) + by_hi * low_axis, col)

    right, left = along(1), along(side - 1)
    peers = [(row, lax.rem(col + k, cols)) for k in range(1, cols)] if flags else []
    barrier = pltpu.get_barrier_semaphore()
    for peer in [right, left, *peers]:
        pl.semaphore_signal(barrier, inc=1, device_id=peer, device_id_type=MESH)
    pl.semaphore_wait(barrier, 2 + len(peers))

    half = send_ref.shape[1] // 2
    lower, upper = pl.ds(0, half), pl.ds(half, half)

    def copy(n, src, dst, peer):
        return pltpu.make_async_remote_copy(
            src_ref=src,
            dst_ref=dst,
            send_sem=send_sem.at[n],
            recv_sem=recv_sem.at[n],
            device_id=peer,
            device_id_type=MESH,
        )

    far_up = copy(0, send_ref.at[1, lower], relay_up, right)
    far_down = copy(1, send_ref.at[1, upper], relay_down, left)
    near_up = copy(2, send_ref.at[0], recv_ref.at[2], right)
    near_down = copy(3, send_ref.at[2], recv_ref.at[0], left)
    next_up = copy(4, relay_up, recv_ref.at[1, lower], right)
    next_down = copy(5, relay_down, recv_ref.at[1, upper], left)
    told = [copy(6 + k, flag_ref, heard_ref.at[k], peer) for k, peer in enumerate(peers)]
    far_up.start()
    far_down.start()
    near_up.start()
    near_down.start()
    for one in told:
        one.start()
    far_up.wait_recv()
    next_up.start()
    far_down.wait_recv()
    next_down.start()
    far_up.wait_send()
    far_down.wait_send()
    for one in told:
        one.wait()
    near_up.wait()
    near_down.wait()
    next_up.wait()
    next_down.wait()


def ring(send, flag, side, cols, stage):
    three, cap, *block = send.shape
    flags = flag is not None
    copies = 6 + (cols - 1 if flags else 0)
    out_shape = [jax.ShapeDtypeStruct(send.shape, send.dtype)]
    if flags:
        out_shape.append(jax.ShapeDtypeStruct((cols - 1, *flag.shape), flag.dtype))
    return pl.pallas_call(
        functools.partial(ring_body, side=side, cols=cols, stage=stage, flags=flags),
        out_shape=out_shape,
        in_specs=[pl.BlockSpec(memory_space=pl.ANY)] * (2 if flags else 1),
        out_specs=[pl.BlockSpec(memory_space=pl.ANY)] * len(out_shape),
        scratch_shapes=[
            pltpu.VMEM((cap // 2, *block), send.dtype),
            pltpu.VMEM((cap // 2, *block), send.dtype),
            pltpu.SemaphoreType.DMA((copies,)),
            pltpu.SemaphoreType.DMA((copies,)),
        ],
        compiler_params=pltpu.CompilerParams(collective_id=stage, has_side_effects=True),
        name="ring",
    )(*([send, flag] if flags else [send]))


def products_body(
    rc_ref, todo_ref, jobs_ref, band_ref, recv1_ref, recv2_ref, out_ref, held, half, acc, cube, jobs, sem, *, per
):
    n_band, n1, n2 = band_ref.shape[0], recv1_ref.shape[0], recv2_ref.shape[0]
    copies = [
        pltpu.make_async_copy(recv2_ref, held.at[pl.ds(n_band + 1 + n1, n2)], sem.at[2]),
        pltpu.make_async_copy(recv1_ref, held.at[pl.ds(n_band + 1, n1)], sem.at[1]),
        pltpu.make_async_copy(band_ref, held.at[pl.ds(0, n_band)], sem.at[0]),
    ]
    for one in copies:
        one.start()
    rows = out_ref.shape[0]
    tile = rows * per
    slots = n_band // rows
    block = out_ref.shape[2:]
    first_own = rc_ref[1] * per
    most = todo_ref[0, 7, 0]
    held[n_band] = jnp.zeros(block, BF16)
    half[n_band] = jnp.zeros(block, BF16)

    @pl.when(most > 2 * LEVELS)
    def _():
        pltpu.sync_copy(jobs_ref, jobs)

    for one in copies:
        one.wait()

    def pair(left, which, m):
        a = [left[todo_ref[which, 2 + 2 * q, m]] for q in range(2)]
        b = [held[todo_ref[which, 3 + 2 * q, m]] for q in range(2)]
        return jnp.dot(
            jnp.concatenate(a, axis=1), jnp.concatenate(b, axis=0), preferred_element_type=F32
        )

    def rest(left, i, t, total):
        g, lane = i // 4, lax.rem(i, 4) * 32 + t

        def step(q, total):
            code = jobs[g, q, lane]
            a = left[i * slots + code // JOB]
            return total + jnp.dot(a, held[lax.rem(code, JOB)], preferred_element_type=F32)

        return lax.fori_loop(2 * LEVELS, jobs[g, slots, lane], step, total)

    for level in range(LEVELS):

        def four(m4, carry, level=level):
            sums = [pair(held, 2 * level, m4 * 4 + k) for k in range(4)]
            for k in range(4):
                at = todo_ref[2 * level, 0, m4 * 4 + k]
                total = sums[k] if level == 0 else acc[at] + sums[k]
                acc[at] = total
                half[at] = total.astype(BF16)
            return carry

        lax.fori_loop(0, (todo_ref[2 * level, 6, 0] + 3) // 4, four, 0)
    half[n_band] = jnp.zeros(block, BF16)

    @pl.when(most > 2 * LEVELS)
    def _():
        def late(n, carry):
            i, t = n // slots, lax.rem(n, slots)

            @pl.when(jobs[i // 4, slots, lax.rem(i, 4) * 32 + t] > 2 * LEVELS)
            def _():
                total = rest(held, i, t, acc[n])
                acc[n] = total
                half[n] = total.astype(BF16)

            return carry

        lax.fori_loop(0, n_band, late, 0)

    for level in range(LEVELS):

        def four_cubes(m4, carry, level=level):
            sums = [pair(half, 2 * level + 1, m4 * 4 + k) for k in range(4)]
            for k in range(4):
                at = todo_ref[2 * level + 1, 1, m4 * 4 + k]
                cube[at] = sums[k] if level == 0 else cube[at] + sums[k]
            return carry

        lax.fori_loop(0, (todo_ref[2 * level + 1, 6, 0] + 3) // 4, four_cubes, 0)

    @pl.when(most > 2 * LEVELS)
    def _():
        def late(n, carry):
            cube[n] = rest(half, n // per, first_own + lax.rem(n, per), cube[n])
            return carry

        lax.fori_loop(0, tile, late, 0)

    for i in range(rows):
        for s in range(per):
            square = acc[i * slots + first_own + s]
            out_ref[i, s] = (3.0 * square - 2.0 * cube[i * per + s]).astype(BF16)


def products(rc, todo, jobs, band, recv1, recv2, rows, per):
    block = band.shape[1:]
    blocks = band.shape[0] + recv1.shape[0] + recv2.shape[0]
    return pl.pallas_call(
        functools.partial(products_body, per=per),
        out_shape=jax.ShapeDtypeStruct((rows, per, *block), BF16),
        in_specs=[pl.BlockSpec(memory_space=pltpu.SMEM)] * 2
        + [pl.BlockSpec(memory_space=pl.ANY)] * 4,
        out_specs=pl.BlockSpec(memory_space=pltpu.VMEM),
        scratch_shapes=[
            pltpu.VMEM((blocks + 1, *block), BF16),
            pltpu.VMEM((band.shape[0] + 1, *block), BF16),
            pltpu.VMEM((band.shape[0] + 1, *block), F32),
            pltpu.VMEM((rows * per + 1, *block), F32),
            pltpu.SMEM(jobs.shape, I32),
            pltpu.SemaphoreType.DMA((3,)),
        ],
        compiler_params=pltpu.CompilerParams(vmem_limit_bytes=60 * 1024 * 1024),
        name="products",
    )(rc, todo, jobs, band, recv1, recv2)


def spread_body(x_ref, out_ref, send_sem, recv_sem, *, axis, size):
    row, col = lax.axis_index("row"), lax.axis_index("col")

    def peer(k):
        if axis == "row":
            return (lax.rem(row + k, size), col)
        return (row, lax.rem(col + k, size))

    barrier = pltpu.get_barrier_semaphore()
    for k in range(1, size):
        pl.semaphore_signal(barrier, inc=1, device_id=peer(k), device_id_type=MESH)
    pl.semaphore_wait(barrier, size - 1)
    copies = []
    for k in range(1, size):
        one = pltpu.make_async_remote_copy(
            src_ref=x_ref,
            dst_ref=out_ref.at[k - 1],
            send_sem=send_sem.at[k - 1],
            recv_sem=recv_sem.at[k - 1],
            device_id=peer(k),
            device_id_type=MESH,
        )
        one.start()
        copies.append(one)
    for one in copies:
        one.wait()


def spread(x, axis, size, collective_id):
    others = pl.pallas_call(
        functools.partial(spread_body, axis=axis, size=size),
        out_shape=jax.ShapeDtypeStruct((size - 1, *x.shape), x.dtype),
        in_specs=[pl.BlockSpec(memory_space=pl.ANY)],
        out_specs=pl.BlockSpec(memory_space=pl.ANY),
        scratch_shapes=[pltpu.SemaphoreType.DMA((size - 1,)), pltpu.SemaphoreType.DMA((size - 1,))],
        compiler_params=pltpu.CompilerParams(collective_id=collective_id, has_side_effects=True),
        name="spread",
    )(x)
    return jnp.concatenate([x[None], others], axis=0)


def dense_body(rc_ref, cols_ref, left_ref, panel_ref, out_ref, left, right, acc, sem, *, dims, mixed):
    side, band_rows, _, per = dims
    slots = cols_ref.shape[1]
    row_here, col_here = rc_ref[0], rc_ref[1]
    tile = band_rows * per
    row_count, col_count = side * side, slots // per

    def one_out(n, carry):
        i, s = n // per, lax.rem(n, per)
        target = cols_ref[row_here * band_rows + i, col_here * per + s]
        acc[...] = jnp.zeros_like(acc)

        def one_t(t, carry):
            k = cols_ref[row_here * band_rows + i, t]
            safe = jnp.maximum(k, 0)
            away = lax.rem(row_here - safe // band_rows + row_count, row_count)
            if mixed:
                back = lax.rem(col_here - t // per + col_count, col_count)
                at_left = back * tile + i * per + lax.rem(t, per)
            else:
                at_left = i * slots + t
            for u in range(per):
                found = cols_ref[safe, col_here * per + u]

                @pl.when((k >= 0) & (target >= 0) & (found == target))
                def _(u=u):
                    at = away * tile + lax.rem(safe, band_rows) * per + u
                    a = pltpu.make_async_copy(left_ref.at[at_left], left, sem.at[0])
                    b = pltpu.make_async_copy(panel_ref.at[at], right, sem.at[1])
                    a.start()
                    b.start()
                    a.wait()
                    b.wait()
                    acc[...] += jnp.dot(left[...], right[...], preferred_element_type=F32)

            return carry

        lax.fori_loop(0, slots, one_t, 0)
        out_ref[n] = acc[...]
        return carry

    lax.fori_loop(0, tile, one_out, 0)


def dense_step(rc, cols, left, panel, dims, mixed):
    _, band_rows, _, per = dims
    block = left.shape[1:]
    return pl.pallas_call(
        functools.partial(dense_body, dims=dims, mixed=mixed),
        out_shape=jax.ShapeDtypeStruct((band_rows * per, *block), F32),
        in_specs=[pl.BlockSpec(memory_space=pltpu.SMEM)] * 2
        + [pl.BlockSpec(memory_space=pl.ANY)] * 2,
        out_specs=pl.BlockSpec(memory_space=pltpu.VMEM),
        scratch_shapes=[
            pltpu.VMEM(block, BF16),
            pltpu.VMEM(block, BF16),
            pltpu.VMEM(block, F32),
            pltpu.SemaphoreType.DMA((2,)),
        ],
        name="dense_step",
    )(rc, cols, left, panel)


def dense(rc, cols, density, dims, sizes):
    _, band_rows, _, per = dims
    rows, slots, *block = density.shape
    row_size, col_size = sizes
    tile = lax.dynamic_slice_in_dim(density, rc[1] * per, per, 1)
    tile = tile.reshape(band_rows * per, *block)
    panel = spread(tile, "row", row_size, 2).reshape(-1, *block)
    square = dense_step(rc, cols, density.reshape(-1, *block), panel, dims, False)
    half = spread(square.astype(BF16), "col", col_size, 3).reshape(-1, *block)
    cube = dense_step(rc, cols, half, panel, dims, True)
    return (3.0 * square - 2.0 * cube).astype(BF16).reshape(rows, per, *block)


def local(density, cols, *, sizes):
    rows, slots, *block = density.shape
    row_size, col_size = sizes
    side = math.isqrt(row_size)
    per = slots // col_size
    width = cols.shape[0] // col_size
    dims = (side, rows, width, per)
    rc = jnp.stack([lax.axis_index("row"), lax.axis_index("col")]).astype(I32)
    band = density.reshape(rows * slots, *block)
    src1, src2, jobs, todo, flag = make_plan(rc, cols, dims)
    near = (side - 1) * CAP1
    far = (side - 1) * CAP2
    packed = gather(src1, near, band)
    recv1, heard = ring(packed.reshape(side - 1, CAP1, *block), flag, side, col_size, 0)
    recv1 = recv1.reshape(near, *block)
    packed = gather(src2, far, recv1, band)
    (recv2,) = ring(packed.reshape(side - 1, CAP2, *block), None, side, col_size, 1)
    recv2 = recv2.reshape(far, *block)
    over = jnp.max(heard) + flag[0, 0] > 0
    return lax.cond(
        over,
        lambda: dense(rc, cols, density, dims, sizes),
        lambda: products(rc, todo, jobs, band, recv1, recv2, rows, per),
    )


def solution(mesh):
    sizes = (mesh.shape["row"], mesh.shape["col"])
    return jax.shard_map(
        functools.partial(local, sizes=sizes),
        mesh=mesh,
        in_specs=(P("row", None, None, None), P()),
        out_specs=P("row", "col", None, None),
        check_vma=False,
    )
```

```python
import functools
import math

import jax
import jax.numpy as jnp
from jax import lax
from jax.experimental import pallas as pl
from jax.experimental.pallas import tpu as pltpu
from jax.sharding import PartitionSpec as P

F32 = jnp.float32
BF16 = jnp.bfloat16
I32 = jnp.int32
CAP1 = 40
CAP2 = 48
JOB = 1024
LEVELS = 4
STEPS1 = (26, 30, 34, CAP1)
STEPS2 = (32, 36, 40, CAP2)
MESH = pl.DeviceIdType.MESH


def fdiv(x, n):
    return jnp.floor((x + 0.5) * (1.0 / n))


def mm(a, b, contract=((1,), (0,))):
    return lax.dot_general(
        a.astype(BF16), b.astype(BF16), (contract, ((), ())), preferred_element_type=F32
    )


NT = ((1,), (1,))


def ones_where(cond):
    return jnp.where(cond, 1.0, 0.0).astype(F32)


def plan_core(
    row_here, col_here, cols_ref, src1_ref, src2_ref, jobs_ref, todo_ref, own_ref, want_ref, part_ref, counted, *, dims
):
    side, band_rows, width, per = dims
    count, slots = cols_ref.shape
    hi_here = row_here // side
    lo_here = lax.rem(row_here, side)
    odd = lax.rem(col_here, 2)
    p_here = jnp.where(odd == 0, lo_here, hi_here)
    q_here = jnp.where(odd == 0, hi_here, lo_here)
    odd_f = odd.astype(F32)
    p_f, q_f = p_here.astype(F32), q_here.astype(F32)

    square = (count, count)
    row_at = lax.broadcasted_iota(I32, square, 0).astype(F32)
    lane_at = lax.broadcasted_iota(I32, square, 1).astype(F32)
    group = fdiv(lane_at, width)

    def coords(index):
        band = fdiv(index, band_rows)
        hi = fdiv(band, side)
        lo = band - side * hi
        p = odd_f * hi + (1.0 - odd_f) * lo
        q = odd_f * lo + (1.0 - odd_f) * hi
        p = p - p_f
        q = q - q_f
        return band, p + side * ones_where(p < 0.0), q + side * ones_where(q < 0.0)

    band, prel, qrel = coords(row_at)
    band_lane, _, qrel_lane = coords(lane_at)
    own_row = row_at - band_rows * band

    slot_row = lax.broadcasted_iota(I32, (slots, count), 0).astype(F32)
    slot_lane = lax.broadcasted_iota(I32, (slots, count), 1).astype(F32)
    cols = cols_ref[...].astype(F32)
    occupied = jnp.zeros(square, F32)
    slot = per * group
    for u in range(per):
        expand = ones_where(slot_row == per * fdiv(slot_lane, width) + u)
        hit = ones_where(mm(cols, expand) == lane_at)
        occupied = occupied + hit
        slot = slot + u * hit
    own_ref[...] = jnp.where(occupied > 0.0, slot, -1.0)

    in_group = ones_where(group == col_here.astype(F32))
    part = occupied * in_group
    shared = mm(part, part, NT)
    wanted = occupied * jnp.maximum(in_group, ones_where(shared > 0.0))
    identity = ones_where(row_at == lane_at)
    flipped = mm(identity, occupied, NT)
    wanted_b = wanted.astype(BF16)
    want_ref[...] = wanted

    def needed_by(d, e):
        pd, qe = lax.rem(p_here + d, side), lax.rem(q_here + e, side)
        who = jnp.where(odd == 0, qe * side + pd, pd * side + qe).astype(F32)
        picked = flipped * ones_where(band_lane == who)
        return occupied * ones_where(mm(picked, wanted_b) > 0.0)

    before = ones_where(row_at < lane_at)
    in_band = ones_where((lane_at < row_at) & (band_lane == band))
    in_class = ones_where((lane_at < row_at) & (qrel_lane == qrel))
    everything = jnp.ones(square, BF16)

    def rank_of(need, earlier):
        return mm(need, before) + mm(mm(earlier, need), everything)

    class_row = lax.broadcasted_iota(I32, (8, count), 0).astype(F32)
    _, _, class_of = coords(lax.broadcasted_iota(I32, (8, count), 1).astype(F32))
    classes = ones_where(class_of == class_row)
    most1 = jnp.zeros((1, count), F32)
    most2 = jnp.zeros((8, 1), F32)
    union, direct = [], []
    for d in range(side):
        total = None
        for e in range(side):
            need = needed_by(d, e)
            sums = jnp.sum(mm(classes, need), axis=1, keepdims=True)
            sums = sums * ones_where(class_row[:, :1] != float(e))
            most2 = jnp.maximum(most2, sums)
            total = need if total is None else jnp.maximum(total, need)
            if d == 0:
                direct.append(need)
        union.append(total)
    rank1, rank2 = [], []
    for d in range(side):
        rank = rank_of(union[d], in_band)
        rank1.append(rank)
        used = (rank + 1.0) * union[d] * ones_where(prel != float(d))
        most1 = jnp.maximum(most1, jnp.max(used, axis=0, keepdims=True))
        rank2.append(rank_of(direct[d], in_class))
    most1 = jnp.max(most1, axis=1, keepdims=True)
    most2 = jnp.max(most2, axis=0, keepdims=True)
    after_counts = counted(most1, most2)

    def tally(need, where):
        kept = jnp.sum(need * where, axis=0, keepdims=True)
        return jnp.sum(kept, axis=1, keepdims=True)

    tallies = [tally(union[0], ones_where((qrel == 0.0) & (prel == float(d)))) for d in range(1, side)]
    tallies += [tally(direct[0], ones_where(qrel == float(e))) for e in range(1, side)]

    def invert(rank, value_hi, value_lo, cap):
        rows = []
        value = 64.0 * value_hi + value_lo + 1.0
        for n in range(cap):
            rows.append(jnp.sum(jnp.where(rank == float(n + 1), value, 0.0), axis=0, keepdims=True))
        return jnp.concatenate(rows, axis=0)

    def to_lanes(stack):
        ones = jnp.ones((8, stack.shape[1]), F32)
        return lax.dot_general(
            ones, stack, (NT, ((), ())), preferred_element_type=F32, precision=lax.Precision.HIGHEST
        )

    sel_row = lax.broadcasted_iota(I32, (16, count), 0).astype(F32)
    sel_lane = lax.broadcasted_iota(I32, (16, count), 1).astype(F32)
    first = (row_here * band_rows).astype(F32)
    pick = ones_where((sel_lane == sel_row + first) & (sel_row < float(band_rows)))
    slot16 = mm(pick, slot)
    place = sel_row * slots + slot16
    zeros16 = jnp.zeros_like(place)
    stacks = []
    for d in range(1, side):
        rank = mm(pick, jnp.minimum((rank1[d] + 1.0) * union[d], 255.0))
        stacks.append(invert(rank, zeros16, place, CAP1))
    src1 = to_lanes(jnp.concatenate(stacks, axis=0))
    src1_ref[...] = src1.astype(I32)

    in_recv1 = (prel - 1.0) * CAP1 + jnp.minimum(rank1[0], CAP1 - 1.0)
    in_band_at = own_row * slots + slot
    after1 = jnp.where(prel == 0.0, (side - 1.0) * CAP1 + in_band_at, in_recv1)
    members = side * band_rows
    mem_row = lax.broadcasted_iota(I32, (members, count), 0).astype(F32)
    mem_lane = lax.broadcasted_iota(I32, (members, count), 1).astype(F32)
    mem_band, mem_p, mem_q = coords(mem_lane)
    pick = ones_where(
        (mem_q == 0.0) & (mem_p * band_rows + (mem_lane - band_rows * mem_band) == mem_row)
    )
    after_hi = fdiv(after1, 64)
    hi48 = mm(pick, after_hi)
    lo48 = mm(pick, after1 - 64.0 * after_hi)
    stacks = []
    for e in range(1, side):
        rank = mm(pick, jnp.minimum((rank2[e] + 1.0) * direct[e], 255.0))
        stacks.append(invert(rank, hi48, lo48, CAP2))
    src2 = to_lanes(jnp.concatenate(stacks, axis=0))
    src2_ref[...] = src2.astype(I32)

    held = band_rows * slots
    loc = jnp.where(
        prel + qrel == 0.0,
        in_band_at,
        jnp.where(
            qrel == 0.0,
            held + 1.0 + in_recv1,
            held + 1.0 + (side - 1.0) * CAP1 + (qrel - 1.0) * CAP2 + jnp.minimum(rank2[0], CAP2 - 1.0),
        ),
    )
    loc_hi = fdiv(loc, 64)
    loc_lo = (loc - 64.0 * loc_hi).astype(BF16)
    loc_hi = loc_hi.astype(BF16)
    occ_b = occupied.astype(BF16)
    small = (slots, count)
    t_at = lax.broadcasted_iota(I32, small, 0).astype(F32)
    wide_at = lax.broadcasted_iota(I32, (128, count), 0).astype(F32)
    pack = 4
    wide_i = fdiv(wide_at, 128 // pack)
    wide_t = wide_at - (128 // pack) * wide_i
    tri = ones_where(
        lax.broadcasted_iota(I32, (slots, slots), 1) < lax.broadcasted_iota(I32, (slots, slots), 0)
    )
    t_out = lax.broadcasted_iota(I32, (slots, 128), 0).astype(F32)
    def one_part(g, carry):
        exists = jnp.zeros((slots, 128), F32)
        at_hi = jnp.zeros((slots, 128), F32)
        at_lo = jnp.zeros((slots, 128), F32)
        flags = jnp.zeros((1, 128), F32)
        for ii in range(pack):
            at_row = row_here * band_rows + g * pack + ii
            line = own_ref[pl.ds(at_row, 1), :]
            left = ones_where(t_at == line).astype(BF16)
            right = ones_where((wide_i == float(ii)) & (wide_t == line))
            right = (right * want_ref[pl.ds(at_row, 1), :]).astype(BF16)
            exists = exists + mm(mm(left, occ_b), right, NT)
            at_hi = at_hi + mm(mm(left, loc_hi), right, NT)
            at_lo = at_lo + mm(mm(left, loc_lo), right, NT)
            flags = flags + mm(jnp.ones((8, count), BF16), right, NT)[:1]
        rank = jnp.where(exists > 0.0, mm(tri, exists), -1.0)
        code = t_out * JOB + at_hi * 64.0 + at_lo
        rows = []
        for n in range(slots):
            rows.append(jnp.sum(jnp.where(rank == float(n), code, 0.0), axis=0, keepdims=True))
        rows.append(jnp.sum(exists, axis=0, keepdims=True))
        rows.append(flags)
        spare = jnp.zeros((32 - slots - 2, 128), F32)
        part_ref[g] = jnp.concatenate([*rows, spare], axis=0)
        jobs_ref[g] = part_ref[g].astype(I32)
        return carry

    groups = band_rows // pack
    lax.fori_loop(0, groups, one_part, 0)
    if after_counts is not None:
        after_counts()

    lanes = 128 * groups
    parts = [part_ref[g] for g in range(groups)]

    def whole(n):
        return jnp.concatenate([rows[n : n + 1] for rows in parts], axis=1)

    at = lax.broadcasted_iota(I32, (1, lanes), 1).astype(F32)
    i_at = fdiv(at, 128 // pack)
    t_of = at - (128 // pack) * i_at
    mine = t_of - per * col_here.astype(F32)
    own = ones_where((mine >= 0.0) & (mine < per))
    number_of = i_at * slots + t_of
    own_at = i_at * per + mine
    n_of = whole(slots)
    needed = jnp.maximum(whole(slots + 1), own)
    upper = ones_where(
        lax.broadcasted_iota(I32, (lanes, lanes), 0) < lax.broadcasted_iota(I32, (lanes, lanes), 1)
    ).astype(BF16)
    place_at = lax.broadcasted_iota(I32, (lanes, lanes), 0).astype(F32)
    slot_here = lax.broadcasted_iota(I32, (1, lanes), 1).astype(F32)
    most = jnp.max(n_of, axis=1, keepdims=True)

    def split(value):
        high = fdiv(value, 64)
        return [high, value - 64.0 * high]

    blank = float(held)
    for level in range(LEVELS):
        codes = [whole(2 * level + q) for q in range(2)]
        fields = split(number_of) + split(own_at * own)
        for q in range(2):
            there = n_of > float(2 * level + q)
            t_left = fdiv(codes[q], JOB)
            fields += split(jnp.where(there, i_at * slots + t_left, blank))
            fields += split(jnp.where(there, codes[q] - JOB * t_left, blank))
        table = jnp.concatenate(fields + [jnp.zeros((4, lanes), F32)], axis=0)
        for kind in range(2):
            mask = own if kind else needed
            if level > 0:
                mask = mask * ones_where(n_of > float(2 * level))
            rank = mm(jnp.broadcast_to(mask, (8, lanes)), upper)[:1]
            rank = jnp.where(mask > 0.0, rank, -1.0)
            packed = mm(table, ones_where(place_at == rank), NT)
            total = jnp.sum(mask, axis=1, keepdims=True)
            valid = slot_here < total
            spare = [blank, float(band_rows * per), blank, blank, blank, blank]
            rows = []
            for f in range(6):
                value = packed[2 * f : 2 * f + 1] * 64.0 + packed[2 * f + 1 : 2 * f + 2]
                rows.append(jnp.where(valid, value, spare[f]))
            rows.append(jnp.broadcast_to(total, (1, lanes)))
            facts = jnp.broadcast_to(most, (1, lanes))
            for k, value in enumerate(tallies):
                facts = jnp.where(slot_here == float(k + 1), value, facts)
            rows.append(facts)
            todo_ref[2 * level + kind] = jnp.concatenate(rows, axis=0).astype(I32)


def plan_body(
    cols_ref,
    src1_ref,
    src2_ref,
    jobs_ref,
    todo_ref,
    over_ref,
    step1_ref,
    step2_ref,
    own_ref,
    want_ref,
    part_ref,
    flag_ref,
    heard_ref,
    send_sem,
    recv_sem,
    *,
    dims,
    col_size,
):
    row, col = lax.axis_index("row"), lax.axis_index("col")
    peers = [(row, lax.rem(col + k, col_size)) for k in range(1, col_size)]
    barrier = pltpu.get_barrier_semaphore()
    for peer in peers:
        pl.semaphore_signal(barrier, inc=1, device_id=peer, device_id_type=MESH)
    pl.semaphore_wait(barrier, col_size - 1)
    told = [
        pltpu.make_async_remote_copy(
            src_ref=flag_ref,
            dst_ref=heard_ref.at[k],
            send_sem=send_sem.at[k],
            recv_sem=recv_sem.at[k],
            device_id=peer,
            device_id_type=MESH,
        )
        for k, peer in enumerate(peers)
    ]

    def counted(most1, most2):
        which = lax.broadcasted_iota(I32, flag_ref.shape, 0)
        flag_ref[...] = jnp.where(which == 0, most1, most2).astype(I32)

        def tell():
            for one in told:
                one.start()

        return tell

    plan_core(
        row, col, cols_ref, src1_ref, src2_ref, jobs_ref, todo_ref, own_ref, want_ref, part_ref, counted, dims=dims
    )
    for one in told:
        one.wait()
    heard = flag_ref[...]
    for k in range(col_size - 1):
        heard = jnp.maximum(heard, heard_ref[k])
    most1 = jnp.max(heard[0:1])
    most2 = jnp.max(heard[1:2])

    def step(most, steps):
        return sum((most > n).astype(I32) for n in steps[:-1])

    over_ref[0] = ((most1 > STEPS1[-1]) | (most2 > STEPS2[-1])).astype(I32)
    step1_ref[0] = step(most1, STEPS1)
    step2_ref[0] = step(most2, STEPS2)


def plan_shapes(dims):
    side, band_rows, _, _ = dims
    groups = band_rows // 4
    return (
        jax.ShapeDtypeStruct((8, (side - 1) * CAP1), I32),
        jax.ShapeDtypeStruct((8, (side - 1) * CAP2), I32),
        jax.ShapeDtypeStruct((groups, 32, 128), I32),
        jax.ShapeDtypeStruct((2 * LEVELS, 8, 128 * groups), I32),
    )


def plan_scratch(dims, count):
    groups = dims[1] // 4
    return [
        pltpu.VMEM((count, count), F32),
        pltpu.VMEM((count, count), F32),
        pltpu.VMEM((groups, 32, 128), F32),
    ]


def make_plan(cols, dims, col_size):
    lists = plan_shapes(dims)
    choice = jax.ShapeDtypeStruct((1,), I32)
    return pl.pallas_call(
        functools.partial(plan_body, dims=dims, col_size=col_size),
        out_shape=(*lists, choice, choice, choice),
        in_specs=[pl.BlockSpec(memory_space=pltpu.VMEM)],
        out_specs=[pl.BlockSpec(memory_space=pltpu.VMEM)] * len(lists)
        + [pl.BlockSpec(memory_space=pltpu.SMEM)] * 3,
        scratch_shapes=[
            *plan_scratch(dims, cols.shape[0]),
            pltpu.VMEM((8, 128), I32),
            pltpu.VMEM((col_size - 1, 8, 128), I32),
            pltpu.SemaphoreType.DMA((col_size - 1,)),
            pltpu.SemaphoreType.DMA((col_size - 1,)),
        ],
        compiler_params=pltpu.CompilerParams(collective_id=0, has_side_effects=True),
        name="plan",
    )(cols)


def gather_body(index_ref, *refs, sizes):
    sources, out_ref, sem = refs[: len(sizes)], refs[len(sizes)], refs[-1]
    total = out_ref.shape[0]

    def issue(n, count):
        at = index_ref[0, n] - 1
        start = 0
        for ref, size in zip(sources, sizes):
            inside = (at >= start) & (at < start + size)

            @pl.when(inside)
            def _(ref=ref, start=start):
                pltpu.make_async_copy(ref.at[at - start], out_ref.at[n], sem).start()

            start += size
        return count + jnp.where(at >= 0, 1, 0)

    count = lax.fori_loop(0, total, issue, jnp.zeros((), I32), unroll=4)

    def settle(n, carry):
        pltpu.make_async_copy(out_ref.at[0], out_ref.at[0], sem).wait()
        return carry

    lax.fori_loop(0, count, settle, 0)


def gather(index, total, *sources):
    block = sources[0].shape[1:]
    return pl.pallas_call(
        functools.partial(gather_body, sizes=tuple(s.shape[0] for s in sources)),
        out_shape=jax.ShapeDtypeStruct((total, *block), sources[0].dtype),
        in_specs=[pl.BlockSpec(memory_space=pltpu.SMEM)]
        + [pl.BlockSpec(memory_space=pl.ANY)] * len(sources),
        out_specs=pl.BlockSpec(memory_space=pltpu.VMEM),
        scratch_shapes=[pltpu.SemaphoreType.DMA],
        name="gather",
    )(index, *sources)


def ring_body(send_ref, recv_ref, relay_up, relay_down, send_sem, recv_sem, *, side, stage, cap):
    row, col = lax.axis_index("row"), lax.axis_index("col")
    hi, lo = row // side, lax.rem(row, side)
    low_axis = lax.rem(col + stage, 2)

    def along(d):
        by_lo = hi * side + lax.rem(lo + d, side)
        by_hi = lax.rem(hi + d, side) * side + lo
        return (by_lo * (1 - low_axis) + by_hi * low_axis, col)

    right, left = along(1), along(side - 1)
    barrier = pltpu.get_barrier_semaphore()
    for peer in (right, left):
        pl.semaphore_signal(barrier, inc=1, device_id=peer, device_id_type=MESH)
    pl.semaphore_wait(barrier, 2)

    half = cap // 2
    lower, upper, both = pl.ds(0, half), pl.ds(half, half), pl.ds(0, cap)

    def copy(n, src, dst, peer):
        return pltpu.make_async_remote_copy(
            src_ref=src,
            dst_ref=dst,
            send_sem=send_sem.at[n],
            recv_sem=recv_sem.at[n],
            device_id=peer,
            device_id_type=MESH,
        )

    far_up = copy(0, send_ref.at[1, lower], relay_up, right)
    far_down = copy(1, send_ref.at[1, upper], relay_down, left)
    near_up = copy(2, send_ref.at[0, both], recv_ref.at[2, both], right)
    near_down = copy(3, send_ref.at[2, both], recv_ref.at[0, both], left)
    next_up = copy(4, relay_up, recv_ref.at[1, lower], right)
    next_down = copy(5, relay_down, recv_ref.at[1, upper], left)
    far_up.start()
    far_down.start()
    near_up.start()
    near_down.start()
    far_up.wait_recv()
    next_up.start()
    far_down.wait_recv()
    next_down.start()
    far_up.wait_send()
    far_down.wait_send()
    near_up.wait()
    near_down.wait()
    next_up.wait()
    next_down.wait()


def ring(send, side, stage, cap, collective_id):
    block = send.shape[2:]
    return pl.pallas_call(
        functools.partial(ring_body, side=side, stage=stage, cap=cap),
        out_shape=jax.ShapeDtypeStruct(send.shape, send.dtype),
        in_specs=[pl.BlockSpec(memory_space=pl.ANY)],
        out_specs=pl.BlockSpec(memory_space=pl.ANY),
        scratch_shapes=[
            pltpu.VMEM((cap // 2, *block), send.dtype),
            pltpu.VMEM((cap // 2, *block), send.dtype),
            pltpu.SemaphoreType.DMA((6,)),
            pltpu.SemaphoreType.DMA((6,)),
        ],
        compiler_params=pltpu.CompilerParams(collective_id=collective_id, has_side_effects=True),
        name="ring",
    )(send)


def ring_of(step, steps, send, side, stage, first_id):
    choices = [
        functools.partial(ring, side=side, stage=stage, cap=cap, collective_id=first_id + n)
        for n, cap in enumerate(steps)
    ]
    return lax.switch(step, choices, send)


def products_body(
    rc_ref, todo_ref, jobs_ref, band_ref, recv1_ref, recv2_ref, out_ref, held, half, acc, cube, jobs, sem, *, per
):
    n_band, n1, n2 = band_ref.shape[0], recv1_ref.shape[0], recv2_ref.shape[0]
    whole_band = pltpu.make_async_copy(band_ref, held.at[pl.ds(0, n_band)], sem.at[0])
    lists, chunk = 3, 8

    def received(action):
        start = n_band + 1
        for which, (ref, size) in enumerate(((recv1_ref, n1), (recv2_ref, n2))):
            cap = size // lists
            for d in range(lists):
                here = todo_ref[0, 7, 1 + which * lists + d]
                for at in range(d * cap, d * cap + cap, chunk):

                    @pl.when(here > at - d * cap)
                    def _(ref=ref, at=at, start=start):
                        span = pl.ds(at, chunk)
                        one = pltpu.make_async_copy(
                            ref.at[span], held.at[pl.ds(start + at, chunk)], sem.at[1]
                        )
                        action(one)

            start += size

    whole_band.start()
    received(lambda one: one.start())
    rows = out_ref.shape[0]
    tile = rows * per
    slots = n_band // rows
    block = out_ref.shape[2:]
    first_own = rc_ref[1] * per
    most = todo_ref[0, 7, 0]
    held[n_band] = jnp.zeros(block, BF16)
    half[n_band] = jnp.zeros(block, BF16)

    @pl.when(most > 2 * LEVELS)
    def _():
        pltpu.sync_copy(jobs_ref, jobs)

    whole_band.wait()
    received(lambda one: one.wait())

    def pair(left, which, m):
        a = [left[todo_ref[which, 2 + 2 * q, m]] for q in range(2)]
        b = [held[todo_ref[which, 3 + 2 * q, m]] for q in range(2)]
        return jnp.dot(
            jnp.concatenate(a, axis=1), jnp.concatenate(b, axis=0), preferred_element_type=F32
        )

    def rest(left, i, t, total):
        g, lane = i // 4, lax.rem(i, 4) * 32 + t

        def step(q, total):
            code = jobs[g, q, lane]
            a = left[i * slots + code // JOB]
            return total + jnp.dot(a, held[lax.rem(code, JOB)], preferred_element_type=F32)

        return lax.fori_loop(2 * LEVELS, jobs[g, slots, lane], step, total)

    for level in range(LEVELS):

        def four(m4, carry, level=level):
            sums = [pair(held, 2 * level, m4 * 4 + k) for k in range(4)]
            for k in range(4):
                at = todo_ref[2 * level, 0, m4 * 4 + k]
                total = sums[k] if level == 0 else acc[at] + sums[k]
                acc[at] = total
                half[at] = total.astype(BF16)
            return carry

        lax.fori_loop(0, (todo_ref[2 * level, 6, 0] + 3) // 4, four, 0)
    half[n_band] = jnp.zeros(block, BF16)

    @pl.when(most > 2 * LEVELS)
    def _():
        def late(n, carry):
            i, t = n // slots, lax.rem(n, slots)

            @pl.when(jobs[i // 4, slots, lax.rem(i, 4) * 32 + t] > 2 * LEVELS)
            def _():
                total = rest(held, i, t, acc[n])
                acc[n] = total
                half[n] = total.astype(BF16)

            return carry

        lax.fori_loop(0, n_band, late, 0)

    for level in range(LEVELS):

        def four_cubes(m4, carry, level=level):
            sums = [pair(half, 2 * level + 1, m4 * 4 + k) for k in range(4)]
            for k in range(4):
                at = todo_ref[2 * level + 1, 1, m4 * 4 + k]
                cube[at] = sums[k] if level == 0 else cube[at] + sums[k]
            return carry

        lax.fori_loop(0, (todo_ref[2 * level + 1, 6, 0] + 3) // 4, four_cubes, 0)

    @pl.when(most > 2 * LEVELS)
    def _():
        def late(n, carry):
            cube[n] = rest(half, n // per, first_own + lax.rem(n, per), cube[n])
            return carry

        lax.fori_loop(0, tile, late, 0)

    for i in range(rows):
        for s in range(per):
            square = acc[i * slots + first_own + s]
            out_ref[i, s] = (3.0 * square - 2.0 * cube[i * per + s]).astype(BF16)


def products(rc, todo, jobs, band, recv1, recv2, rows, per):
    block = band.shape[1:]
    blocks = band.shape[0] + recv1.shape[0] + recv2.shape[0]
    return pl.pallas_call(
        functools.partial(products_body, per=per),
        out_shape=jax.ShapeDtypeStruct((rows, per, *block), BF16),
        in_specs=[pl.BlockSpec(memory_space=pltpu.SMEM)] * 2
        + [pl.BlockSpec(memory_space=pl.ANY)] * 4,
        out_specs=pl.BlockSpec(memory_space=pltpu.VMEM),
        scratch_shapes=[
            pltpu.VMEM((blocks + 1, *block), BF16),
            pltpu.VMEM((band.shape[0] + 1, *block), BF16),
            pltpu.VMEM((band.shape[0] + 1, *block), F32),
            pltpu.VMEM((rows * per + 1, *block), F32),
            pltpu.SMEM(jobs.shape, I32),
            pltpu.SemaphoreType.DMA((2,)),
        ],
        compiler_params=pltpu.CompilerParams(vmem_limit_bytes=60 * 1024 * 1024),
        name="products",
    )(rc, todo, jobs, band, recv1, recv2)


def spread_body(x_ref, out_ref, send_sem, recv_sem, *, axis, size):
    row, col = lax.axis_index("row"), lax.axis_index("col")

    def peer(k):
        if axis == "row":
            return (lax.rem(row + k, size), col)
        return (row, lax.rem(col + k, size))

    barrier = pltpu.get_barrier_semaphore()
    for k in range(1, size):
        pl.semaphore_signal(barrier, inc=1, device_id=peer(k), device_id_type=MESH)
    pl.semaphore_wait(barrier, size - 1)
    copies = []
    for k in range(1, size):
        one = pltpu.make_async_remote_copy(
            src_ref=x_ref,
            dst_ref=out_ref.at[k - 1],
            send_sem=send_sem.at[k - 1],
            recv_sem=recv_sem.at[k - 1],
            device_id=peer(k),
            device_id_type=MESH,
        )
        one.start()
        copies.append(one)
    for one in copies:
        one.wait()


def spread(x, axis, size, collective_id):
    others = pl.pallas_call(
        functools.partial(spread_body, axis=axis, size=size),
        out_shape=jax.ShapeDtypeStruct((size - 1, *x.shape), x.dtype),
        in_specs=[pl.BlockSpec(memory_space=pl.ANY)],
        out_specs=pl.BlockSpec(memory_space=pl.ANY),
        scratch_shapes=[pltpu.SemaphoreType.DMA((size - 1,)), pltpu.SemaphoreType.DMA((size - 1,))],
        compiler_params=pltpu.CompilerParams(collective_id=collective_id, has_side_effects=True),
        name="spread",
    )(x)
    return jnp.concatenate([x[None], others], axis=0)


def dense_body(rc_ref, cols_ref, left_ref, panel_ref, out_ref, left, right, acc, sem, *, dims, mixed):
    side, band_rows, _, per = dims
    slots = cols_ref.shape[1]
    row_here, col_here = rc_ref[0], rc_ref[1]
    tile = band_rows * per
    row_count, col_count = side * side, slots // per

    def one_out(n, carry):
        i, s = n // per, lax.rem(n, per)
        target = cols_ref[row_here * band_rows + i, col_here * per + s]
        acc[...] = jnp.zeros_like(acc)

        def one_t(t, carry):
            k = cols_ref[row_here * band_rows + i, t]
            safe = jnp.maximum(k, 0)
            away = lax.rem(row_here - safe // band_rows + row_count, row_count)
            if mixed:
                back = lax.rem(col_here - t // per + col_count, col_count)
                at_left = back * tile + i * per + lax.rem(t, per)
            else:
                at_left = i * slots + t
            for u in range(per):
                found = cols_ref[safe, col_here * per + u]

                @pl.when((k >= 0) & (target >= 0) & (found == target))
                def _(u=u):
                    at = away * tile + lax.rem(safe, band_rows) * per + u
                    a = pltpu.make_async_copy(left_ref.at[at_left], left, sem.at[0])
                    b = pltpu.make_async_copy(panel_ref.at[at], right, sem.at[1])
                    a.start()
                    b.start()
                    a.wait()
                    b.wait()
                    acc[...] += jnp.dot(left[...], right[...], preferred_element_type=F32)

            return carry

        lax.fori_loop(0, slots, one_t, 0)
        out_ref[n] = acc[...]
        return carry

    lax.fori_loop(0, tile, one_out, 0)


def dense_step(rc, cols, left, panel, dims, mixed):
    _, band_rows, _, per = dims
    block = left.shape[1:]
    return pl.pallas_call(
        functools.partial(dense_body, dims=dims, mixed=mixed),
        out_shape=jax.ShapeDtypeStruct((band_rows * per, *block), F32),
        in_specs=[pl.BlockSpec(memory_space=pltpu.SMEM)] * 2
        + [pl.BlockSpec(memory_space=pl.ANY)] * 2,
        out_specs=pl.BlockSpec(memory_space=pltpu.VMEM),
        scratch_shapes=[
            pltpu.VMEM(block, BF16),
            pltpu.VMEM(block, BF16),
            pltpu.VMEM(block, F32),
            pltpu.SemaphoreType.DMA((2,)),
        ],
        name="dense_step",
    )(rc, cols, left, panel)


def dense(rc, cols, density, dims, sizes):
    _, band_rows, _, per = dims
    rows, slots, *block = density.shape
    row_size, col_size = sizes
    tile = lax.dynamic_slice_in_dim(density, rc[1] * per, per, 1)
    tile = tile.reshape(band_rows * per, *block)
    panel = spread(tile, "row", row_size, 1).reshape(-1, *block)
    square = dense_step(rc, cols, density.reshape(-1, *block), panel, dims, False)
    half = spread(square.astype(BF16), "col", col_size, 2).reshape(-1, *block)
    cube = dense_step(rc, cols, half, panel, dims, True)
    return (3.0 * square - 2.0 * cube).astype(BF16).reshape(rows, per, *block)


def local(density, cols, *, sizes):
    rows, slots, *block = density.shape
    row_size, col_size = sizes
    side = math.isqrt(row_size)
    per = slots // col_size
    width = cols.shape[0] // col_size
    dims = (side, rows, width, per)
    rc = jnp.stack([lax.axis_index("row"), lax.axis_index("col")]).astype(I32)
    band = density.reshape(rows * slots, *block)
    src1, src2, jobs, todo, over, step1, step2 = make_plan(cols, dims, col_size)
    near = (side - 1) * CAP1
    far = (side - 1) * CAP2

    def sparse():
        packed = gather(src1, near, band).reshape(side - 1, CAP1, *block)
        recv1 = ring_of(step1[0], STEPS1, packed, side, 0, 3).reshape(near, *block)
        packed = gather(src2, far, recv1, band).reshape(side - 1, CAP2, *block)
        recv2 = ring_of(step2[0], STEPS2, packed, side, 1, 3 + len(STEPS1)).reshape(far, *block)
        return products(rc, todo, jobs, band, recv1, recv2, rows, per)

    return lax.cond(over[0] > 0, lambda: dense(rc, cols, density, dims, sizes), sparse)


def solution(mesh):
    sizes = (mesh.shape["row"], mesh.shape["col"])
    return jax.shard_map(
        functools.partial(local, sizes=sizes),
        mesh=mesh,
        in_specs=(P("row", None, None, None), P()),
        out_specs=P("row", "col", None, None),
        check_vma=False,
    )
```

```python
import functools
import math

import jax
import jax.numpy as jnp
from jax import lax
from jax.experimental import pallas as pl
from jax.experimental.pallas import tpu as pltpu
from jax.sharding import PartitionSpec as P

F32 = jnp.float32
BF16 = jnp.bfloat16
I32 = jnp.int32
CAP1 = 40
CAP2 = 48
JOB = 1024
LEVELS = 4
STEPS1 = (20, 22, 24, 26, 28, 30, 32, 34, CAP1)
STEPS2 = (24, 26, 28, 30, 32, 34, 36, 40, CAP2)
MESH = pl.DeviceIdType.MESH


def fdiv(x, n):
    return jnp.floor((x + 0.5) * (1.0 / n))


def mm(a, b, contract=((1,), (0,))):
    return lax.dot_general(
        a.astype(BF16), b.astype(BF16), (contract, ((), ())), preferred_element_type=F32
    )


NT = ((1,), (1,))


def ones_where(cond):
    return jnp.where(cond, 1.0, 0.0).astype(F32)


def plan_core(
    row_here, col_here, cols_ref, src1_ref, src2_ref, jobs_ref, todo_ref, own_ref, want_ref, part_ref, counted, *, dims
):
    side, band_rows, width, per = dims
    count, slots = cols_ref.shape
    hi_here = row_here // side
    lo_here = lax.rem(row_here, side)
    odd = lax.rem(col_here, 2)
    p_here = jnp.where(odd == 0, lo_here, hi_here)
    q_here = jnp.where(odd == 0, hi_here, lo_here)
    odd_f = odd.astype(F32)
    p_f, q_f = p_here.astype(F32), q_here.astype(F32)

    square = (count, count)
    row_at = lax.broadcasted_iota(I32, square, 0).astype(F32)
    lane_at = lax.broadcasted_iota(I32, square, 1).astype(F32)
    group = fdiv(lane_at, width)

    def coords(index):
        band = fdiv(index, band_rows)
        hi = fdiv(band, side)
        lo = band - side * hi
        p = odd_f * hi + (1.0 - odd_f) * lo
        q = odd_f * lo + (1.0 - odd_f) * hi
        p = p - p_f
        q = q - q_f
        return band, p + side * ones_where(p < 0.0), q + side * ones_where(q < 0.0)

    band, prel, qrel = coords(row_at)
    band_lane, _, qrel_lane = coords(lane_at)
    own_row = row_at - band_rows * band

    slot_row = lax.broadcasted_iota(I32, (slots, count), 0).astype(F32)
    slot_lane = lax.broadcasted_iota(I32, (slots, count), 1).astype(F32)
    cols = cols_ref[...].astype(F32)
    occupied = jnp.zeros(square, F32)
    slot = per * group
    for u in range(per):
        expand = ones_where(slot_row == per * fdiv(slot_lane, width) + u)
        hit = ones_where(mm(cols, expand) == lane_at)
        occupied = occupied + hit
        slot = slot + u * hit
    own_ref[...] = jnp.where(occupied > 0.0, slot, -1.0)

    in_group = ones_where(group == col_here.astype(F32))
    part = occupied * in_group
    shared = mm(part, part, NT)
    wanted = occupied * jnp.maximum(in_group, ones_where(shared > 0.0))
    identity = ones_where(row_at == lane_at)
    flipped = mm(identity, occupied, NT)
    wanted_b = wanted.astype(BF16)
    want_ref[...] = wanted

    def needed_by(d, e):
        pd, qe = lax.rem(p_here + d, side), lax.rem(q_here + e, side)
        who = jnp.where(odd == 0, qe * side + pd, pd * side + qe).astype(F32)
        picked = flipped * ones_where(band_lane == who)
        return occupied * ones_where(mm(picked, wanted_b) > 0.0)

    before = ones_where(row_at < lane_at)
    in_band = ones_where((lane_at < row_at) & (band_lane == band))
    in_class = ones_where((lane_at < row_at) & (qrel_lane == qrel))
    everything = jnp.ones(square, BF16)

    def rank_of(need, earlier):
        return mm(need, before) + mm(mm(earlier, need), everything)

    class_row = lax.broadcasted_iota(I32, (8, count), 0).astype(F32)
    _, _, class_of = coords(lax.broadcasted_iota(I32, (8, count), 1).astype(F32))
    classes = ones_where(class_of == class_row)
    most1 = jnp.zeros((1, count), F32)
    most2 = jnp.zeros((8, 1), F32)
    union, direct = [], []
    for d in range(side):
        total = None
        for e in range(side):
            need = needed_by(d, e)
            sums = jnp.sum(mm(classes, need), axis=1, keepdims=True)
            sums = sums * ones_where(class_row[:, :1] != float(e))
            most2 = jnp.maximum(most2, sums)
            total = need if total is None else jnp.maximum(total, need)
            if d == 0:
                direct.append(need)
        union.append(total)
    rank1, rank2 = [], []
    for d in range(side):
        rank = rank_of(union[d], in_band)
        rank1.append(rank)
        used = (rank + 1.0) * union[d] * ones_where(prel != float(d))
        most1 = jnp.maximum(most1, jnp.max(used, axis=0, keepdims=True))
        rank2.append(rank_of(direct[d], in_class))
    most1 = jnp.max(most1, axis=1, keepdims=True)
    most2 = jnp.max(most2, axis=0, keepdims=True)
    after_counts = counted(most1, most2)

    def tally(need, where):
        kept = jnp.sum(need * where, axis=0, keepdims=True)
        return jnp.sum(kept, axis=1, keepdims=True)

    tallies = [tally(union[0], ones_where((qrel == 0.0) & (prel == float(d)))) for d in range(1, side)]
    tallies += [tally(direct[0], ones_where(qrel == float(e))) for e in range(1, side)]

    def invert(rank, value_hi, value_lo, cap):
        rows = []
        value = 64.0 * value_hi + value_lo + 1.0
        for n in range(cap):
            rows.append(jnp.sum(jnp.where(rank == float(n + 1), value, 0.0), axis=0, keepdims=True))
        return jnp.concatenate(rows, axis=0)

    def to_lanes(stack):
        ones = jnp.ones((8, stack.shape[1]), F32)
        return lax.dot_general(
            ones, stack, (NT, ((), ())), preferred_element_type=F32, precision=lax.Precision.HIGHEST
        )

    sel_row = lax.broadcasted_iota(I32, (16, count), 0).astype(F32)
    sel_lane = lax.broadcasted_iota(I32, (16, count), 1).astype(F32)
    first = (row_here * band_rows).astype(F32)
    pick = ones_where((sel_lane == sel_row + first) & (sel_row < float(band_rows)))
    slot16 = mm(pick, slot)
    place = sel_row * slots + slot16
    zeros16 = jnp.zeros_like(place)
    stacks = []
    for d in range(1, side):
        rank = mm(pick, jnp.minimum((rank1[d] + 1.0) * union[d], 255.0))
        stacks.append(invert(rank, zeros16, place, CAP1))
    src1 = to_lanes(jnp.concatenate(stacks, axis=0))
    src1_ref[...] = src1.astype(I32)

    in_recv1 = (prel - 1.0) * CAP1 + jnp.minimum(rank1[0], CAP1 - 1.0)
    in_band_at = own_row * slots + slot
    after1 = jnp.where(prel == 0.0, (side - 1.0) * CAP1 + in_band_at, in_recv1)
    members = side * band_rows
    mem_row = lax.broadcasted_iota(I32, (members, count), 0).astype(F32)
    mem_lane = lax.broadcasted_iota(I32, (members, count), 1).astype(F32)
    mem_band, mem_p, mem_q = coords(mem_lane)
    pick = ones_where(
        (mem_q == 0.0) & (mem_p * band_rows + (mem_lane - band_rows * mem_band) == mem_row)
    )
    after_hi = fdiv(after1, 64)
    hi48 = mm(pick, after_hi)
    lo48 = mm(pick, after1 - 64.0 * after_hi)
    stacks = []
    for e in range(1, side):
        rank = mm(pick, jnp.minimum((rank2[e] + 1.0) * direct[e], 255.0))
        stacks.append(invert(rank, hi48, lo48, CAP2))
    src2 = to_lanes(jnp.concatenate(stacks, axis=0))
    src2_ref[...] = src2.astype(I32)

    held = band_rows * slots
    loc = jnp.where(
        prel + qrel == 0.0,
        in_band_at,
        jnp.where(
            qrel == 0.0,
            held + 1.0 + in_recv1,
            held + 1.0 + (side - 1.0) * CAP1 + (qrel - 1.0) * CAP2 + jnp.minimum(rank2[0], CAP2 - 1.0),
        ),
    )
    loc_hi = fdiv(loc, 64)
    loc_lo = (loc - 64.0 * loc_hi).astype(BF16)
    loc_hi = loc_hi.astype(BF16)
    occ_b = occupied.astype(BF16)
    small = (slots, count)
    t_at = lax.broadcasted_iota(I32, small, 0).astype(F32)
    wide_at = lax.broadcasted_iota(I32, (128, count), 0).astype(F32)
    pack = 4
    wide_i = fdiv(wide_at, 128 // pack)
    wide_t = wide_at - (128 // pack) * wide_i
    tri = ones_where(
        lax.broadcasted_iota(I32, (slots, slots), 1) < lax.broadcasted_iota(I32, (slots, slots), 0)
    )
    t_out = lax.broadcasted_iota(I32, (slots, 128), 0).astype(F32)
    def one_part(g, carry):
        exists = jnp.zeros((slots, 128), F32)
        at_hi = jnp.zeros((slots, 128), F32)
        at_lo = jnp.zeros((slots, 128), F32)
        flags = jnp.zeros((1, 128), F32)
        for ii in range(pack):
            at_row = row_here * band_rows + g * pack + ii
            line = own_ref[pl.ds(at_row, 1), :]
            left = ones_where(t_at == line).astype(BF16)
            right = ones_where((wide_i == float(ii)) & (wide_t == line))
            right = (right * want_ref[pl.ds(at_row, 1), :]).astype(BF16)
            exists = exists + mm(mm(left, occ_b), right, NT)
            at_hi = at_hi + mm(mm(left, loc_hi), right, NT)
            at_lo = at_lo + mm(mm(left, loc_lo), right, NT)
            flags = flags + mm(jnp.ones((8, count), BF16), right, NT)[:1]
        rank = jnp.where(exists > 0.0, mm(tri, exists), -1.0)
        code = t_out * JOB + at_hi * 64.0 + at_lo
        rows = []
        for n in range(slots):
            rows.append(jnp.sum(jnp.where(rank == float(n), code, 0.0), axis=0, keepdims=True))
        rows.append(jnp.sum(exists, axis=0, keepdims=True))
        rows.append(flags)
        spare = jnp.zeros((32 - slots - 2, 128), F32)
        part_ref[g] = jnp.concatenate([*rows, spare], axis=0)
        jobs_ref[g] = part_ref[g].astype(I32)
        return carry

    groups = band_rows // pack
    lax.fori_loop(0, groups, one_part, 0)
    if after_counts is not None:
        after_counts()

    lanes = 128 * groups
    parts = [part_ref[g] for g in range(groups)]

    def whole(n):
        return jnp.concatenate([rows[n : n + 1] for rows in parts], axis=1)

    at = lax.broadcasted_iota(I32, (1, lanes), 1).astype(F32)
    i_at = fdiv(at, 128 // pack)
    t_of = at - (128 // pack) * i_at
    mine = t_of - per * col_here.astype(F32)
    own = ones_where((mine >= 0.0) & (mine < per))
    number_of = i_at * slots + t_of
    own_at = i_at * per + mine
    n_of = whole(slots)
    needed = jnp.maximum(whole(slots + 1), own)
    upper = ones_where(
        lax.broadcasted_iota(I32, (lanes, lanes), 0) < lax.broadcasted_iota(I32, (lanes, lanes), 1)
    ).astype(BF16)
    place_at = lax.broadcasted_iota(I32, (lanes, lanes), 0).astype(F32)
    slot_here = lax.broadcasted_iota(I32, (1, lanes), 1).astype(F32)
    most = jnp.max(n_of, axis=1, keepdims=True)

    def split(value):
        high = fdiv(value, 64)
        return [high, value - 64.0 * high]

    blank = float(held)
    for level in range(LEVELS):
        codes = [whole(2 * level + q) for q in range(2)]
        fields = split(number_of) + split(own_at * own)
        for q in range(2):
            there = n_of > float(2 * level + q)
            t_left = fdiv(codes[q], JOB)
            fields += split(jnp.where(there, i_at * slots + t_left, blank))
            fields += split(jnp.where(there, codes[q] - JOB * t_left, blank))
        table = jnp.concatenate(fields + [jnp.zeros((4, lanes), F32)], axis=0)
        for kind in range(2):
            mask = own if kind else needed
            if level > 0:
                mask = mask * ones_where(n_of > float(2 * level))
            rank = mm(jnp.broadcast_to(mask, (8, lanes)), upper)[:1]
            rank = jnp.where(mask > 0.0, rank, -1.0)
            packed = mm(table, ones_where(place_at == rank), NT)
            total = jnp.sum(mask, axis=1, keepdims=True)
            valid = slot_here < total
            spare = [blank, float(band_rows * per), blank, blank, blank, blank]
            rows = []
            for f in range(6):
                value = packed[2 * f : 2 * f + 1] * 64.0 + packed[2 * f + 1 : 2 * f + 2]
                rows.append(jnp.where(valid, value, spare[f]))
            rows.append(jnp.broadcast_to(total, (1, lanes)))
            facts = jnp.broadcast_to(most, (1, lanes))
            for k, value in enumerate(tallies):
                facts = jnp.where(slot_here == float(k + 1), value, facts)
            rows.append(facts)
            todo_ref[2 * level + kind] = jnp.concatenate(rows, axis=0).astype(I32)


def plan_body(
    cols_hbm,
    src1_ref,
    src2_ref,
    jobs_ref,
    todo_ref,
    over_ref,
    step1_ref,
    step2_ref,
    own_ref,
    want_ref,
    part_ref,
    cols_ref,
    cols_sem,
    flag_ref,
    heard_ref,
    send_sem,
    recv_sem,
    *,
    dims,
    col_size,
):
    fetch = pltpu.make_async_copy(cols_hbm, cols_ref, cols_sem)
    fetch.start()
    row, col = lax.axis_index("row"), lax.axis_index("col")
    peers = [(row, lax.rem(col + k, col_size)) for k in range(1, col_size)]
    barrier = pltpu.get_barrier_semaphore()
    for peer in peers:
        pl.semaphore_signal(barrier, inc=1, device_id=peer, device_id_type=MESH)
    pl.semaphore_wait(barrier, col_size - 1)
    told = [
        pltpu.make_async_remote_copy(
            src_ref=flag_ref,
            dst_ref=heard_ref.at[k],
            send_sem=send_sem.at[k],
            recv_sem=recv_sem.at[k],
            device_id=peer,
            device_id_type=MESH,
        )
        for k, peer in enumerate(peers)
    ]

    def counted(most1, most2):
        which = lax.broadcasted_iota(I32, flag_ref.shape, 0)
        flag_ref[...] = jnp.where(which == 0, most1, most2).astype(I32)

        def tell():
            for one in told:
                one.start()

        return tell

    fetch.wait()
    plan_core(
        row, col, cols_ref, src1_ref, src2_ref, jobs_ref, todo_ref, own_ref, want_ref, part_ref, counted, dims=dims
    )
    for one in told:
        one.wait()
    heard = flag_ref[...]
    for k in range(col_size - 1):
        heard = jnp.maximum(heard, heard_ref[k])
    most1 = jnp.max(heard[0:1])
    most2 = jnp.max(heard[1:2])

    def step(most, steps):
        return sum((most > n).astype(I32) for n in steps[:-1])

    own = flag_ref[...]
    over_ref[0] = ((most1 > STEPS1[-1]) | (most2 > STEPS2[-1])).astype(I32)
    step1_ref[0] = step(jnp.max(own[0:1]), STEPS1)
    step2_ref[0] = step(jnp.max(own[1:2]), STEPS2)


def plan_shapes(dims):
    side, band_rows, _, _ = dims
    groups = band_rows // 4
    return (
        jax.ShapeDtypeStruct((8, (side - 1) * CAP1), I32),
        jax.ShapeDtypeStruct((8, (side - 1) * CAP2), I32),
        jax.ShapeDtypeStruct((groups, 32, 128), I32),
        jax.ShapeDtypeStruct((2 * LEVELS, 8, 128 * groups), I32),
    )


def plan_scratch(dims, count):
    groups = dims[1] // 4
    return [
        pltpu.VMEM((count, count), F32),
        pltpu.VMEM((count, count), F32),
        pltpu.VMEM((groups, 32, 128), F32),
    ]


def make_plan(cols, dims, col_size):
    lists = plan_shapes(dims)
    choice = jax.ShapeDtypeStruct((1,), I32)
    return pl.pallas_call(
        functools.partial(plan_body, dims=dims, col_size=col_size),
        out_shape=(*lists, choice, choice, choice),
        in_specs=[pl.BlockSpec(memory_space=pl.ANY)],
        out_specs=[pl.BlockSpec(memory_space=pltpu.VMEM)] * len(lists)
        + [pl.BlockSpec(memory_space=pltpu.SMEM)] * 3,
        scratch_shapes=[
            *plan_scratch(dims, cols.shape[0]),
            pltpu.VMEM(cols.shape, I32),
            pltpu.SemaphoreType.DMA,
            pltpu.VMEM((8, 128), I32),
            pltpu.VMEM((col_size - 1, 8, 128), I32),
            pltpu.SemaphoreType.DMA((col_size - 1,)),
            pltpu.SemaphoreType.DMA((col_size - 1,)),
        ],
        compiler_params=pltpu.CompilerParams(collective_id=0, has_side_effects=True),
        name="plan",
    )(cols)


def gather_body(index_ref, *refs, sizes):
    sources, out_ref, sem = refs[: len(sizes)], refs[len(sizes)], refs[-1]
    total = out_ref.shape[0]

    def issue(n, count):
        at = index_ref[0, n] - 1
        start = 0
        for ref, size in zip(sources, sizes):
            inside = (at >= start) & (at < start + size)

            @pl.when(inside)
            def _(ref=ref, start=start):
                pltpu.make_async_copy(ref.at[at - start], out_ref.at[n], sem).start()

            start += size
        return count + jnp.where(at >= 0, 1, 0)

    count = lax.fori_loop(0, total, issue, jnp.zeros((), I32), unroll=4)

    def settle(n, carry):
        pltpu.make_async_copy(out_ref.at[0], out_ref.at[0], sem).wait()
        return carry

    lax.fori_loop(0, count, settle, 0)


def gather(index, total, *sources):
    block = sources[0].shape[1:]
    return pl.pallas_call(
        functools.partial(gather_body, sizes=tuple(s.shape[0] for s in sources)),
        out_shape=jax.ShapeDtypeStruct((total, *block), sources[0].dtype),
        in_specs=[pl.BlockSpec(memory_space=pltpu.SMEM)]
        + [pl.BlockSpec(memory_space=pl.ANY)] * len(sources),
        out_specs=pl.BlockSpec(memory_space=pltpu.VMEM),
        scratch_shapes=[pltpu.SemaphoreType.DMA],
        name="gather",
    )(index, *sources)


def ring_body(send_ref, recv_ref, relay_up, relay_down, send_sem, recv_sem, *, side, stage, cap):
    row, col = lax.axis_index("row"), lax.axis_index("col")
    hi, lo = row // side, lax.rem(row, side)
    low_axis = lax.rem(col + stage, 2)

    def along(d):
        by_lo = hi * side + lax.rem(lo + d, side)
        by_hi = lax.rem(hi + d, side) * side + lo
        return (by_lo * (1 - low_axis) + by_hi * low_axis, col)

    right, left = along(1), along(side - 1)
    barrier = pltpu.get_barrier_semaphore()
    for peer in (right, left):
        pl.semaphore_signal(barrier, inc=1, device_id=peer, device_id_type=MESH)
    pl.semaphore_wait(barrier, 2)

    half = cap // 2
    lower, upper, both = pl.ds(0, half), pl.ds(half, half), pl.ds(0, cap)

    def copy(n, src, dst, peer):
        return pltpu.make_async_remote_copy(
            src_ref=src,
            dst_ref=dst,
            send_sem=send_sem.at[n],
            recv_sem=recv_sem.at[n],
            device_id=peer,
            device_id_type=MESH,
        )

    far_up = copy(0, send_ref.at[1, lower], relay_up, right)
    far_down = copy(1, send_ref.at[1, upper], relay_down, left)
    near_up = copy(2, send_ref.at[0, both], recv_ref.at[2, both], right)
    near_down = copy(3, send_ref.at[2, both], recv_ref.at[0, both], left)
    next_up = copy(4, relay_up, recv_ref.at[1, lower], right)
    next_down = copy(5, relay_down, recv_ref.at[1, upper], left)
    far_up.start()
    far_down.start()
    near_up.start()
    near_down.start()
    far_up.wait_recv()
    next_up.start()
    far_down.wait_recv()
    next_down.start()
    far_up.wait_send()
    far_down.wait_send()
    near_up.wait()
    near_down.wait()
    next_up.wait()
    next_down.wait()


def ring(send, side, stage, cap, collective_id):
    block = send.shape[2:]
    return pl.pallas_call(
        functools.partial(ring_body, side=side, stage=stage, cap=cap),
        out_shape=jax.ShapeDtypeStruct(send.shape, send.dtype),
        in_specs=[pl.BlockSpec(memory_space=pl.ANY)],
        out_specs=pl.BlockSpec(memory_space=pl.ANY),
        scratch_shapes=[
            pltpu.VMEM((cap // 2, *block), send.dtype),
            pltpu.VMEM((cap // 2, *block), send.dtype),
            pltpu.SemaphoreType.DMA((6,)),
            pltpu.SemaphoreType.DMA((6,)),
        ],
        compiler_params=pltpu.CompilerParams(collective_id=collective_id, has_side_effects=True),
        name="ring",
    )(send)


def ring_of(step, steps, send, side, stage, first_id):
    choices = [
        functools.partial(ring, side=side, stage=stage, cap=cap, collective_id=first_id + n)
        for n, cap in enumerate(steps)
    ]
    return lax.switch(step, choices, send)


def products_body(
    rc_ref, todo_ref, jobs_ref, band_ref, recv1_ref, recv2_ref, out_ref, held, half, acc, cube, jobs, sem, *, per
):
    n_band, n1, n2 = band_ref.shape[0], recv1_ref.shape[0], recv2_ref.shape[0]
    whole_band = pltpu.make_async_copy(band_ref, held.at[pl.ds(0, n_band)], sem.at[0])
    lists, chunk = 3, 8

    def received(action):
        start = n_band + 1
        for which, (ref, size) in enumerate(((recv1_ref, n1), (recv2_ref, n2))):
            cap = size // lists
            for d in range(lists):
                here = todo_ref[0, 7, 1 + which * lists + d]
                for at in range(d * cap, d * cap + cap, chunk):

                    @pl.when(here > at - d * cap)
                    def _(ref=ref, at=at, start=start):
                        span = pl.ds(at, chunk)
                        one = pltpu.make_async_copy(
                            ref.at[span], held.at[pl.ds(start + at, chunk)], sem.at[1]
                        )
                        action(one)

            start += size

    whole_band.start()
    received(lambda one: one.start())
    rows = out_ref.shape[0]
    tile = rows * per
    slots = n_band // rows
    block = out_ref.shape[2:]
    first_own = rc_ref[1] * per
    most = todo_ref[0, 7, 0]
    held[n_band] = jnp.zeros(block, BF16)
    half[n_band] = jnp.zeros(block, BF16)

    @pl.when(most > 2 * LEVELS)
    def _():
        pltpu.sync_copy(jobs_ref, jobs)

    whole_band.wait()
    received(lambda one: one.wait())

    def pair(left, which, m):
        a = [left[todo_ref[which, 2 + 2 * q, m]] for q in range(2)]
        b = [held[todo_ref[which, 3 + 2 * q, m]] for q in range(2)]
        return jnp.dot(
            jnp.concatenate(a, axis=1), jnp.concatenate(b, axis=0), preferred_element_type=F32
        )

    def rest(left, i, t, total):
        g, lane = i // 4, lax.rem(i, 4) * 32 + t

        def step(q, total):
            code = jobs[g, q, lane]
            a = left[i * slots + code // JOB]
            return total + jnp.dot(a, held[lax.rem(code, JOB)], preferred_element_type=F32)

        return lax.fori_loop(2 * LEVELS, jobs[g, slots, lane], step, total)

    for level in range(LEVELS):

        def four(m4, carry, level=level):
            sums = [pair(held, 2 * level, m4 * 4 + k) for k in range(4)]
            for k in range(4):
                at = todo_ref[2 * level, 0, m4 * 4 + k]
                total = sums[k] if level == 0 else acc[at] + sums[k]
                acc[at] = total
                half[at] = total.astype(BF16)
            return carry

        lax.fori_loop(0, (todo_ref[2 * level, 6, 0] + 3) // 4, four, 0)
    half[n_band] = jnp.zeros(block, BF16)

    @pl.when(most > 2 * LEVELS)
    def _():
        def late(n, carry):
            i, t = n // slots, lax.rem(n, slots)

            @pl.when(jobs[i // 4, slots, lax.rem(i, 4) * 32 + t] > 2 * LEVELS)
            def _():
                total = rest(held, i, t, acc[n])
                acc[n] = total
                half[n] = total.astype(BF16)

            return carry

        lax.fori_loop(0, n_band, late, 0)

    for level in range(LEVELS):

        def four_cubes(m4, carry, level=level):
            sums = [pair(half, 2 * level + 1, m4 * 4 + k) for k in range(4)]
            for k in range(4):
                at = todo_ref[2 * level + 1, 1, m4 * 4 + k]
                cube[at] = sums[k] if level == 0 else cube[at] + sums[k]
            return carry

        lax.fori_loop(0, (todo_ref[2 * level + 1, 6, 0] + 3) // 4, four_cubes, 0)

    @pl.when(most > 2 * LEVELS)
    def _():
        def late(n, carry):
            cube[n] = rest(half, n // per, first_own + lax.rem(n, per), cube[n])
            return carry

        lax.fori_loop(0, tile, late, 0)

    for i in range(rows):
        for s in range(per):
            square = acc[i * slots + first_own + s]
            out_ref[i, s] = (3.0 * square - 2.0 * cube[i * per + s]).astype(BF16)


def products(rc, todo, jobs, band, recv1, recv2, rows, per):
    block = band.shape[1:]
    blocks = band.shape[0] + recv1.shape[0] + recv2.shape[0]
    return pl.pallas_call(
        functools.partial(products_body, per=per),
        out_shape=jax.ShapeDtypeStruct((rows, per, *block), BF16),
        in_specs=[pl.BlockSpec(memory_space=pltpu.SMEM)] * 2
        + [pl.BlockSpec(memory_space=pl.ANY)] * 4,
        out_specs=pl.BlockSpec(memory_space=pltpu.VMEM),
        scratch_shapes=[
            pltpu.VMEM((blocks + 1, *block), BF16),
            pltpu.VMEM((band.shape[0] + 1, *block), BF16),
            pltpu.VMEM((band.shape[0] + 1, *block), F32),
            pltpu.VMEM((rows * per + 1, *block), F32),
            pltpu.SMEM(jobs.shape, I32),
            pltpu.SemaphoreType.DMA((2,)),
        ],
        compiler_params=pltpu.CompilerParams(vmem_limit_bytes=60 * 1024 * 1024),
        name="products",
    )(rc, todo, jobs, band, recv1, recv2)


def spread_body(x_ref, out_ref, send_sem, recv_sem, *, axis, size):
    row, col = lax.axis_index("row"), lax.axis_index("col")

    def peer(k):
        if axis == "row":
            return (lax.rem(row + k, size), col)
        return (row, lax.rem(col + k, size))

    barrier = pltpu.get_barrier_semaphore()
    for k in range(1, size):
        pl.semaphore_signal(barrier, inc=1, device_id=peer(k), device_id_type=MESH)
    pl.semaphore_wait(barrier, size - 1)
    copies = []
    for k in range(1, size):
        one = pltpu.make_async_remote_copy(
            src_ref=x_ref,
            dst_ref=out_ref.at[k - 1],
            send_sem=send_sem.at[k - 1],
            recv_sem=recv_sem.at[k - 1],
            device_id=peer(k),
            device_id_type=MESH,
        )
        one.start()
        copies.append(one)
    for one in copies:
        one.wait()


def spread(x, axis, size, collective_id):
    others = pl.pallas_call(
        functools.partial(spread_body, axis=axis, size=size),
        out_shape=jax.ShapeDtypeStruct((size - 1, *x.shape), x.dtype),
        in_specs=[pl.BlockSpec(memory_space=pl.ANY)],
        out_specs=pl.BlockSpec(memory_space=pl.ANY),
        scratch_shapes=[pltpu.SemaphoreType.DMA((size - 1,)), pltpu.SemaphoreType.DMA((size - 1,))],
        compiler_params=pltpu.CompilerParams(collective_id=collective_id, has_side_effects=True),
        name="spread",
    )(x)
    return jnp.concatenate([x[None], others], axis=0)


def dense_body(rc_ref, cols_ref, left_ref, panel_ref, out_ref, left, right, acc, sem, *, dims, mixed):
    side, band_rows, _, per = dims
    slots = cols_ref.shape[1]
    row_here, col_here = rc_ref[0], rc_ref[1]
    tile = band_rows * per
    row_count, col_count = side * side, slots // per

    def one_out(n, carry):
        i, s = n // per, lax.rem(n, per)
        target = cols_ref[row_here * band_rows + i, col_here * per + s]
        acc[...] = jnp.zeros_like(acc)

        def one_t(t, carry):
            k = cols_ref[row_here * band_rows + i, t]
            safe = jnp.maximum(k, 0)
            away = lax.rem(row_here - safe // band_rows + row_count, row_count)
            if mixed:
                back = lax.rem(col_here - t // per + col_count, col_count)
                at_left = back * tile + i * per + lax.rem(t, per)
            else:
                at_left = i * slots + t
            for u in range(per):
                found = cols_ref[safe, col_here * per + u]

                @pl.when((k >= 0) & (target >= 0) & (found == target))
                def _(u=u):
                    at = away * tile + lax.rem(safe, band_rows) * per + u
                    a = pltpu.make_async_copy(left_ref.at[at_left], left, sem.at[0])
                    b = pltpu.make_async_copy(panel_ref.at[at], right, sem.at[1])
                    a.start()
                    b.start()
                    a.wait()
                    b.wait()
                    acc[...] += jnp.dot(left[...], right[...], preferred_element_type=F32)

            return carry

        lax.fori_loop(0, slots, one_t, 0)
        out_ref[n] = acc[...]
        return carry

    lax.fori_loop(0, tile, one_out, 0)


def dense_step(rc, cols, left, panel, dims, mixed):
    _, band_rows, _, per = dims
    block = left.shape[1:]
    return pl.pallas_call(
        functools.partial(dense_body, dims=dims, mixed=mixed),
        out_shape=jax.ShapeDtypeStruct((band_rows * per, *block), F32),
        in_specs=[pl.BlockSpec(memory_space=pltpu.SMEM)] * 2
        + [pl.BlockSpec(memory_space=pl.ANY)] * 2,
        out_specs=pl.BlockSpec(memory_space=pltpu.VMEM),
        scratch_shapes=[
            pltpu.VMEM(block, BF16),
            pltpu.VMEM(block, BF16),
            pltpu.VMEM(block, F32),
            pltpu.SemaphoreType.DMA((2,)),
        ],
        name="dense_step",
    )(rc, cols, left, panel)


def dense(rc, cols, density, dims, sizes):
    _, band_rows, _, per = dims
    rows, slots, *block = density.shape
    row_size, col_size = sizes
    tile = lax.dynamic_slice_in_dim(density, rc[1] * per, per, 1)
    tile = tile.reshape(band_rows * per, *block)
    panel = spread(tile, "row", row_size, 1).reshape(-1, *block)
    square = dense_step(rc, cols, density.reshape(-1, *block), panel, dims, False)
    half = spread(square.astype(BF16), "col", col_size, 2).reshape(-1, *block)
    cube = dense_step(rc, cols, half, panel, dims, True)
    return (3.0 * square - 2.0 * cube).astype(BF16).reshape(rows, per, *block)


def local(density, cols, *, sizes):
    rows, slots, *block = density.shape
    row_size, col_size = sizes
    side = math.isqrt(row_size)
    per = slots // col_size
    width = cols.shape[0] // col_size
    dims = (side, rows, width, per)
    rc = jnp.stack([lax.axis_index("row"), lax.axis_index("col")]).astype(I32)
    band = density.reshape(rows * slots, *block)
    src1, src2, jobs, todo, over, step1, step2 = make_plan(cols, dims, col_size)
    near = (side - 1) * CAP1
    far = (side - 1) * CAP2

    def sparse():
        packed = gather(src1, near, band).reshape(side - 1, CAP1, *block)
        recv1 = ring_of(step1[0], STEPS1, packed, side, 0, 3).reshape(near, *block)
        packed = gather(src2, far, recv1, band).reshape(side - 1, CAP2, *block)
        recv2 = ring_of(step2[0], STEPS2, packed, side, 1, 3 + len(STEPS1)).reshape(far, *block)
        return products(rc, todo, jobs, band, recv1, recv2, rows, per)

    return lax.cond(over[0] > 0, lambda: dense(rc, cols, density, dims, sizes), sparse)


def solution(mesh):
    sizes = (mesh.shape["row"], mesh.shape["col"])
    return jax.shard_map(
        functools.partial(local, sizes=sizes),
        mesh=mesh,
        in_specs=(P("row", None, None, None), P()),
        out_specs=P("row", "col", None, None),
        check_vma=False,
    )
```
